1024 devices in a mesh: tm: 16 (over y, x_lo, core), space: 64 (over z, x_hi).
Axes of the slice: x: 4 (x_hi: 2, x_lo: 2; x = x_hi * 2 + x_lo), y: 4, z: 32, core: 2. Of those that a mesh axis runs over, the one named last changes fastest.
Arguments:
- dilution: int32 [8, 2], replicated, may hold values from 0 to 63, as said below
- eigvecs: float32 [2, 3, 16, 64, 13824], P(None, None, 'tm', None, 'space'), may hold values from -6 to 6
- gauge_links: float32 [16, 4, 2, 3, 3, 13824], P('tm', None, None, None, None, 'space'), may hold values from -2.4 to 2.4
- clover: float32 [16, 2, 2, 6, 6, 13824], P('tm', None, None, None, None, 'space'), may hold values from -0.14 to 1.34
Outputs:
- solutions: float32 [2, 4, 3, 16, 8, 13824], P(None, None, None, 'tm', None, 'space')
- perambulator: float32 [16, 64, 2, 4, 8], P('tm', 'space')
The draws below stay inside these ranges and needn't reach their ends.
Inputs may be any that keep to these rules, and one draw needn't show every extreme that they name: `dilution`: column 0 of row s is the eigenvector of source s and column 1 its spin, 0 to 3; some row names eigenvector 64 - 1.
All inputs are finite; a program needn't handle non-finite values.
Results may differ from the reference program's by a relative error of at most 0.0003.
Values sent between devices are 32-bit elements; how exact they have to be, the bound alone decides.
No kernel may reach another device: no remote copies, remote signals or barrier semaphores. Data moves between devices by JAX's collectives and lax.ppermute only.
A program may use at most 128 MiB of HBM per device.

```python
import jax
import jax.numpy as jnp
import numpy as np
from jax import lax

LX = 6
SRC = 8
NEV = 64
ITERS = 3
NT = 16
SIDE = 4
TILES = 64
LS = 216
VOLUME = 13824


def draw_dilution(key, part):
    first, second, third = jax.random.split(jax.random.fold_in(key, 11), 3)
    eigen_index = jax.random.randint(first, (SRC,), 0, NEV)
    spin_index = jax.random.randint(second, (SRC,), 0, 4)
    pinned = jax.random.randint(third, (), 0, SRC)
    eigen_index = jnp.where(jnp.arange(SRC) == pinned, NEV - 1, eigen_index)
    return jnp.stack([eigen_index, spin_index], axis=1).astype(jnp.int32)


def draw_clover(key, part):
    first, second = jax.random.split(jax.random.fold_in(key, 23), 2)
    shape = (NT, 2, 2, 6, 6, VOLUME)
    raw = jax.random.uniform(first, shape, jnp.float32, -1.0, 1.0)
    herm_real = raw[:, 0] + jnp.swapaxes(raw[:, 0], 2, 3)
    herm_imag = raw[:, 1] - jnp.swapaxes(raw[:, 1], 2, 3)
    lift = jax.random.uniform(second, (NT, 2, 6, VOLUME), jnp.float32, 0.0, 1.0)
    identity = jnp.eye(6, dtype=jnp.float32)[None, None, :, :, None]
    real_part = 0.07 * herm_real + identity * (1.0 + 0.2 * lift[:, :, :, None])
    imag_part = 0.07 * herm_imag
    return jnp.stack([real_part, imag_part], axis=1).astype(jnp.float32)


def level_of(stream_key, dims, pieces, smallest, high):
    level, own = 1.0, jax.random.fold_in(stream_key, 6)
    for position, blocks in pieces:
        steps = jnp.exp(jax.random.uniform(jax.random.fold_in(own, position), (blocks,), jnp.float32, smallest / len(pieces), high / len(pieces)))
        level = level * jnp.repeat(steps, dims[position] // blocks).reshape([-1 if axis == position else 1 for axis in range(len(dims))])
    return level


def bell_draw(rng, shape, scale, bound, cuts=(), kind=jnp.bfloat16):
    loudness = level_of(rng, shape, cuts, -0.22, 0.18) if cuts else 1.0
    drawn = jax.random.normal(rng, shape, jnp.float32) * scale * loudness
    return jnp.minimum(jnp.maximum(drawn, -bound), bound).astype(kind)


def setup_inputs(seed: int = 0) -> dict:
    key_of = jax.random.split(jax.random.key(seed), 5)
    dilution = draw_dilution(jax.random.fold_in(key_of[4], 71), 0)
    eigvecs = bell_draw(key_of[1], (2, 3, NT, NEV, VOLUME), 1.0, 6.0, ((2, 16), (4, 64)), jnp.float32)
    gauge_links = bell_draw(key_of[2], (NT, 4, 2, 3, 3, VOLUME), 0.4, 2.4, ((0, 16), (5, 64)), jnp.float32)
    clover = draw_clover(jax.random.fold_in(key_of[4], 71), 0)
    return {"dilution": dilution, "eigvecs": eigvecs, "gauge_links": gauge_links, "clover": clover}


HOPPING = 0.125
RELAXATION = (0.9, 1.0, 1.1)
SPIN_BLOCKS = (
    ((0.0, -1j), (-1j, 0.0)),
    ((0.0, -1.0), (1.0, 0.0)),
    ((-1j, 0.0), (0.0, 1j)),
    ((1.0, 0.0), (0.0, 1.0)),
)


def scaled(factor, real_part, imag_part):
    factor_real = factor.real
    factor_imag = factor.imag
    if factor_imag == 0.0:
        return factor_real * real_part, factor_real * imag_part
    if factor_real == 0.0:
        return -factor_imag * imag_part, factor_imag * real_part
    return factor_real * real_part - factor_imag * imag_part, factor_real * imag_part + factor_imag * real_part


def mirrored(value):
    entry = complex(value)
    return complex(entry.real, -entry.imag)


def dagger_of(matrix):
    return [[mirrored(matrix[column_index][row_index]) for column_index in range(2)] for row_index in range(2)]


def spin_block(matrix, values):
    rows_real = []
    rows_imag = []
    for row_index in range(2):
        summed_real = None
        summed_imag = None
        for column_index in range(2):
            factor = complex(matrix[row_index][column_index])
            if factor == 0:
                continue
            part_real, part_imag = scaled(factor, values[0, column_index], values[1, column_index])
            if summed_real is None:
                summed_real, summed_imag = part_real, part_imag
            else:
                summed_real = summed_real + part_real
                summed_imag = summed_imag + part_imag
        rows_real.append(summed_real)
        rows_imag.append(summed_imag)
    return jnp.stack([jnp.stack(rows_real), jnp.stack(rows_imag)])


def project(spinor, direction, parity):
    moved = spin_block(SPIN_BLOCKS[direction], spinor[:, 2:4])
    return spinor[:, 0:2] + parity * moved


def rebuild(halves, direction, parity):
    lower = parity * spin_block(dagger_of(SPIN_BLOCKS[direction]), halves)
    return jnp.concatenate([halves, lower], axis=1)


def color_times(gauge, values, adjoint):
    link_real = gauge[0]
    link_imag = gauge[1]
    if adjoint:
        link_real = jnp.swapaxes(link_real, 0, 1)
        link_imag = -jnp.swapaxes(link_imag, 0, 1)
    out_real = 0.0
    out_imag = 0.0
    for column_index in range(3):
        left_real = link_real[:, column_index][None, :, None]
        left_imag = link_imag[:, column_index][None, :, None]
        right_real = values[0][:, column_index][:, None]
        right_imag = values[1][:, column_index][:, None]
        out_real = out_real + left_real * right_real - left_imag * right_imag
        out_imag = out_imag + left_real * right_imag + left_imag * right_real
    return jnp.stack([out_real, out_imag])


def clover_times(clover, spinor):
    blocks = []
    for chiral in range(2):
        piece = spinor[:, 2 * chiral:2 * chiral + 2]
        shape = piece.shape
        flat = piece.reshape((2, 6) + shape[3:])
        out_real = 0.0
        out_imag = 0.0
        for column_index in range(6):
            left_real = clover[0, chiral, :, column_index][:, None]
            left_imag = clover[1, chiral, :, column_index][:, None]
            right_real = flat[0, column_index][None]
            right_imag = flat[1, column_index][None]
            out_real = out_real + left_real * right_real - left_imag * right_imag
            out_imag = out_imag + left_real * right_imag + left_imag * right_real
        blocks.append(jnp.stack([out_real, out_imag]).reshape(shape))
    return jnp.concatenate(blocks, axis=1)


def block_order():
    return np.array([number ^ (number >> 1) for number in range(SIDE)], np.int32)


def to_grid(array):
    leading = array.shape[:-2]
    depth = len(leading)
    shaped = array.reshape(leading + (SIDE, SIDE, SIDE, LX, LX, LX))
    for offset in range(3):
        shaped = jnp.take(shaped, block_order(), axis=depth + offset)
    layout = tuple(range(depth)) + (depth, depth + 3, depth + 1, depth + 4, depth + 2, depth + 5)
    return jnp.transpose(shaped, layout).reshape(leading + (SIDE * LX, SIDE * LX, SIDE * LX))


def from_grid(array):
    leading = array.shape[:-3]
    depth = len(leading)
    shaped = array.reshape(leading + (SIDE, LX, SIDE, LX, SIDE, LX))
    layout = tuple(range(depth)) + (depth, depth + 2, depth + 4, depth + 1, depth + 3, depth + 5)
    shaped = jnp.transpose(shaped, layout)
    for offset in range(3):
        shaped = jnp.take(shaped, block_order(), axis=depth + offset)
    return shaped.reshape(leading + (SIDE ** 3, LX ** 3))


def grid_hop(spinor, links_grid):
    summed = 0.0
    axes_of = (5, 6, 7, 4)
    for direction in range(4):
        gauge = links_grid[direction]
        ahead = jnp.roll(spinor, -1, axis=axes_of[direction])
        moved = color_times(gauge, ahead, False)
        forward = rebuild(project(moved, direction, -1.0), direction, -1.0)
        carried = color_times(gauge, spinor, True)
        behind = jnp.roll(carried, 1, axis=axes_of[direction])
        backward = rebuild(project(behind, direction, 1.0), direction, 1.0)
        summed = summed + forward + backward
    return summed


def reference(dilution, eigvecs, gauge_links, clover):
    basis = jnp.transpose(eigvecs, (3, 0, 1, 2, 4)).reshape((NEV, 2, 3, NT, TILES, LS))
    links_old = jnp.moveaxis(gauge_links, 0, 4).reshape((4, 2, 3, 3, NT, TILES, LS))
    clover_old = jnp.moveaxis(clover, 0, 4).reshape((2, 2, 6, 6, NT, TILES, LS))
    links_grid = to_grid(links_old)
    clover_grid = to_grid(clover_old)

    def solve_one(entry):
        chosen = jnp.take(basis, entry[0], axis=0)
        spin_mask = (jnp.arange(4) == entry[1]).astype(jnp.float32).reshape(1, 4, 1, 1, 1, 1, 1)
        source = spin_mask * chosen[:, None, :, None]
        source = to_grid(source)
        spinor = source
        for section in range(ITERS):
            applied = clover_times(clover_grid, spinor) - HOPPING * grid_hop(spinor, links_grid)
            spinor = spinor + RELAXATION[section % 3] * (source - applied)
        return from_grid(spinor)[:, :, :, 0]

    solved = lax.map(solve_one, dilution)
    solutions = jnp.moveaxis(solved, 0, 3)
    precise = lax.Precision.HIGHEST

    def contract(left, right):
        return jnp.einsum("lctgx,acstgx->tlas", left, right, precision=precise)

    basis_real = basis[:, 0]
    basis_imag = basis[:, 1]
    real_sum = contract(basis_real, solutions[0]) + contract(basis_imag, solutions[1])
    imag_sum = contract(basis_real, solutions[1]) - contract(basis_imag, solutions[0])
    perambulator = jnp.stack([real_sum, imag_sum], axis=2) * (1.0 / (3.0 * VOLUME))
    solutions_out = jnp.swapaxes(solutions, 3, 4).reshape((2, 4, 3, NT, SRC, VOLUME))
    return solutions_out, perambulator
```

```python
import functools

import jax
import jax.numpy as jnp
from jax import lax
from jax.experimental import pallas as pl
from jax.experimental.pallas import tpu as pltpu
from jax.sharding import PartitionSpec as P

HOPPING = 0.125
RELAXATION = (0.9, 1.0, 1.1)
SITES = 216
LANES = 256
STRIDES = (36, 6, 1)
SPIN_BLOCKS = (
    ((0.0, -1j), (-1j, 0.0)),
    ((0.0, -1.0), (1.0, 0.0)),
    ((-1j, 0.0), (0.0, 1j)),
    ((1.0, 0.0), (0.0, 1.0)),
)
F32 = jnp.float32


def half(part, spin, colour):
    return (part * 2 + spin) * 3 + colour


def full(part, spin, colour):
    return (part * 4 + spin) * 3 + colour


def rotated(value, shift):
    shift %= LANES
    return value if shift == 0 else pltpu.roll(value, shift, axis=value.ndim - 1)


def add_turned(base, factor, real, imag):
    if factor == 1:
        return base[0] + real, base[1] + imag
    if factor == -1:
        return base[0] - real, base[1] - imag
    if factor == 1j:
        return base[0] - imag, base[1] + real
    return base[0] + imag, base[1] - real


def project(get, direction, parity):
    out = {}
    for spin in range(2):
        row = SPIN_BLOCKS[direction][spin]
        column = 0 if row[0] != 0 else 1
        factor = complex(parity * row[column])
        for colour in range(3):
            base = (get(0, spin, colour), get(1, spin, colour))
            real, imag = add_turned(base, factor, get(0, 2 + column, colour), get(1, 2 + column, colour))
            out[half(0, spin, colour)] = real
            out[half(1, spin, colour)] = imag
    return out


def rebuild(total, values, direction, parity):
    for spin in range(2):
        for colour in range(3):
            for part in range(2):
                q = full(part, spin, colour)
                total[q] = total[q] + values[half(part, spin, colour)]
    for spin in range(2):
        column = 0 if SPIN_BLOCKS[direction][0][spin] != 0 else 1
        factor = complex(parity * complex(SPIN_BLOCKS[direction][column][spin]).conjugate())
        for colour in range(3):
            q, r = full(0, 2 + spin, colour), full(1, 2 + spin, colour)
            total[q], total[r] = add_turned(
                (total[q], total[r]), factor, values[half(0, column, colour)], values[half(1, column, colour)]
            )


def link(links, direction, part, row, column):
    at = ((direction * 3 + row) * 3 + column) * 2 + part
    return jnp.broadcast_to(links[at : at + 1, :], (8, LANES))


def color_times(links, direction, values, adjoint):
    out = {}
    for row in range(3):
        for spin in range(2):
            real = imag = None
            for column in range(3):
                at = (column, row) if adjoint else (row, column)
                u_real = link(links, direction, 0, *at)
                u_imag = link(links, direction, 1, *at)
                v_real, v_imag = values[half(0, spin, column)], values[half(1, spin, column)]
                if adjoint:
                    a = u_real * v_real + u_imag * v_imag
                    b = u_real * v_imag - u_imag * v_real
                else:
                    a = u_real * v_real - u_imag * v_imag
                    b = u_real * v_imag + u_imag * v_real
                real = a if real is None else real + a
                imag = b if imag is None else imag + b
            out[half(0, spin, row)] = real
            out[half(1, spin, row)] = imag
    return out


def lane_slots():
    lane = lax.broadcasted_iota(jnp.int32, (8, LANES), 1)
    sixth = lane * 10923 >> 16
    x = sixth * 10923 >> 16
    return x, sixth - 6 * x, lane - 6 * sixth


def even_bits(dimension):
    bits = lax.axis_index("space") >> 2 * (2 - dimension)
    return ((bits ^ bits >> 1) & 1) == 0


def emit_messages(get, links, carried, sends, last_t):
    slots = lane_slots()
    for direction in range(3):
        stride, slot = STRIDES[direction], slots[direction]
        ahead_is_low_bit = even_bits(direction)
        forward = project(get, direction, -1)
        backward = color_times(links, direction, project(get, direction, 1), True)
        for q in range(12):
            carried[direction * 12 + q] = backward[q]
        for vector in range(2):
            low = forward[6 * vector]
            high = rotated(backward[6 * vector], -5 * stride)
            for r in range(1, 6):
                low = jnp.where(slot == r, rotated(forward[6 * vector + r], stride * r), low)
                high = jnp.where(slot == r, rotated(backward[6 * vector + r], stride * (r - 5)), high)
            first = jnp.where(ahead_is_low_bit, high, low)
            second = jnp.where(ahead_is_low_bit, low, high)
            if direction == 0:
                number = lax.axis_index("space") >> 4
                sends[0][number, vector] = jnp.zeros_like(first)
                sends[0][number ^ 3, vector] = jnp.zeros_like(first)
                sends[0][number ^ 1, vector] = first
                sends[0][number ^ 2, vector] = second
            else:
                sends[2 * direction - 1][vector] = first
                sends[2 * direction][vector] = second
    forward = project(get, 3, -1)
    backward = color_times(links, 3, project(get, 3, 1), True)
    for q in range(12):
        sends[5][q] = forward[q]
        sends[6][q] = backward[q]


def column_of(row):
    square = (8, 8)
    same = lax.broadcasted_iota(jnp.int32, square, 0) == lax.broadcasted_iota(jnp.int32, square, 1)
    return jnp.sum(jnp.where(same, jnp.broadcast_to(row.astype(F32), square), 0.0), axis=1, keepdims=True)


def source_getter(chosen, dilution):
    spins = jnp.broadcast_to(column_of(dilution[1:2, :]), (8, LANES))
    masks = [(spins == spin).astype(F32) for spin in range(4)]

    def get(part, spin, colour):
        return masks[spin] * chosen[part * 3 + colour]

    return get


def start_kernel(dilution, eigvecs, gauge, chosen, links, carried, *sends):
    links[...] = jnp.zeros_like(links)
    for direction in range(4):
        for row in range(3):
            for column in range(3):
                at = ((direction * 3 + row) * 3 + column) * 2
                links[at : at + 2, 0:SITES] = gauge[direction, row, column]
    chosen[...] = jnp.zeros_like(chosen)
    pick = (lax.broadcasted_iota(jnp.int32, (8, 64), 1) == jnp.broadcast_to(column_of(dilution[0:1, :]), (8, 64)).astype(jnp.int32)).astype(F32)
    for part in range(2):
        for colour in range(3):
            chosen[part * 3 + colour, :, 0:SITES] = lax.dot(
                pick, eigvecs[part, colour], precision=lax.Precision.HIGHEST, preferred_element_type=F32
            )
    emit_messages(source_getter(chosen, dilution), links, carried, sends, None)


def clover_kernel(clover, packed):
    packed[...] = jnp.zeros_like(packed)
    for part in range(2):
        for row in range(6):
            for column in range(6):
                at = ((part * 6 + row) * 6 + column) * 2
                packed[at : at + 2, 0:SITES] = clover[part, row, column]


def step(weight, get, source, links, clover, carried, received, total, store):
    total[...] = jnp.zeros_like(total)
    slots = lane_slots()
    for direction in range(3):
        stride, slot = STRIDES[direction], slots[direction]
        ahead_is_low_bit = even_bits(direction)
        if direction == 0:
            number = lax.axis_index("space") >> 4
            first, second = received[0][number ^ 1], received[0][number ^ 2]
        else:
            first, second = received[2 * direction - 1], received[2 * direction]
        ahead = [jnp.where(ahead_is_low_bit, first[v], second[v]) for v in range(2)]
        behind = [jnp.where(ahead_is_low_bit, second[v], first[v]) for v in range(2)]
        forward = project(get, direction, -1)
        for q in range(12):
            v, r = divmod(q, 6)
            forward[q] = jnp.where(
                slot == 5, rotated(ahead[v], stride * (5 - r)), rotated(forward[q], -stride)
            )
        rebuild(total, color_times(links, direction, forward, False), direction, -1)
        backward = {}
        for q in range(12):
            v, r = divmod(q, 6)
            backward[q] = jnp.where(
                slot == 0, rotated(behind[v], -stride * r), rotated(carried[direction * 12 + q], stride)
            )
        rebuild(total, backward, direction, 1)
    rebuild(total, color_times(links, 3, received[5], False), 3, -1)
    rebuild(total, received[6], 3, 1)
    for chiral in range(2):
        for row in range(6):
            real = imag = None
            for column in range(6):
                at = (row * 6 + column) * 2 + chiral
                a_real = jnp.broadcast_to(clover[at : at + 1, :], (8, LANES))
                a_imag = jnp.broadcast_to(clover[72 + at : 73 + at, :], (8, LANES))
                spin, colour = 2 * chiral + column // 3, column % 3
                v_real, v_imag = get(0, spin, colour), get(1, spin, colour)
                a = a_real * v_real - a_imag * v_imag
                b = a_real * v_imag + a_imag * v_real
                real = a if real is None else real + a
                imag = b if imag is None else imag + b
            spin, colour = 2 * chiral + row // 3, row % 3
            for part, applied in ((0, real), (1, imag)):
                q = full(part, spin, colour)
                store(
                    q,
                    get(part, spin, colour)
                    + weight * (source(part, spin, colour) - (applied - HOPPING * total[q])),
                )


def middle_kernel(weight, first, dilution, chosen, links, clover, *rest):
    if first:
        (carried_in, *received), (psi, carried, *sends), total = rest[:8], rest[8:17], rest[17]
        get = source_getter(chosen, dilution)
    else:
        (spinor, carried_in, *received), (psi, carried, *sends), total = rest[:9], rest[9:18], rest[18]
        get = lambda part, spin, colour: spinor[full(part, spin, colour)]

    def store(q, value):
        psi[q] = value

    step(weight, get, source_getter(chosen, dilution), links, clover, carried_in, received, total, store)
    emit_messages(lambda part, spin, colour: psi[full(part, spin, colour)], links, carried, sends, None)


def last_kernel(weight, dilution, chosen, links, clover, eigvecs, spinor, carried, *rest):
    received, (solutions, partial), total = rest[:7], rest[7:9], rest[9]
    get = lambda part, spin, colour: spinor[full(part, spin, colour)]

    def store(q, value):
        solutions[q] = value[:, 0:SITES]

    step(weight, get, source_getter(chosen, dilution), links, clover, carried, received, total, store)
    summed = None
    for colour in range(3):
        real = [solutions[full(0, spin, colour)] for spin in range(4)]
        imag = [solutions[full(1, spin, colour)] for spin in range(4)]
        for part, rows in ((0, real + imag), (1, imag + [-value for value in real])):
            product = lax.dot_general(
                eigvecs[part, colour],
                jnp.concatenate(rows, axis=0),
                (((1,), (1,)), ((), ())),
                precision=lax.Precision.HIGHEST,
                preferred_element_type=F32,
            )
            summed = product if summed is None else summed + product
    partial[...] = summed


def call(kernel, name, outs, args, scratch=()):
    vmem = pl.BlockSpec(memory_space=pltpu.VMEM)
    return pl.pallas_call(
        kernel,
        name=name,
        out_shape=[jax.ShapeDtypeStruct(shape, F32) for shape in outs],
        in_specs=[vmem] * len(args),
        out_specs=[vmem] * len(outs),
        scratch_shapes=scratch,
        compiler_params=pltpu.CompilerParams(vmem_limit_bytes=12 << 20),
    )(*args)


FACE = (2, 8, LANES)
SLICE = (12, 8, LANES)
FIELD = (24, 8, LANES)
CARRIED = (36, 8, LANES)
SENDS = [(4,) + FACE] + [FACE] * 4 + [SLICE] * 2
BITS = (None, 2, 3, 0, 1)
ORDER = (2, 1, 4, 3)


def exchanged(sends):
    size, length = lax.axis_size("space"), lax.axis_size("tm")
    received = [None] * 7
    lines = [[i + 16 * n for n in range(4)] for i in range(16)]
    received[0] = lax.all_to_all(sends[0], "space", 0, 0, axis_index_groups=lines, tiled=True)
    for n in ORDER:
        flip = [(i, i ^ 1 << BITS[n]) for i in range(size)]
        received[n] = lax.ppermute(sends[n], "space", flip)
    received[5] = lax.ppermute(sends[5], "tm", [(i, (i - 1) % length) for i in range(length)])
    received[6] = lax.ppermute(sends[6], "tm", [(i, (i + 1) % length) for i in range(length)])
    return received


def body(dilution, eigvecs, gauge_links, clover):
    eigvecs = eigvecs[:, :, 0]
    dilution = dilution.T
    gauge_links = gauge_links.transpose(0, 1, 3, 4, 2, 5)
    clover = clover.transpose(0, 1, 3, 4, 2, 5)
    total = [pltpu.VMEM(FIELD, F32)]
    chosen, links, carried, *sends = call(
        start_kernel, "start", [(6, 8, LANES), (72, LANES), CARRIED] + SENDS, (dilution, eigvecs, gauge_links[0])
    )
    (packed,) = call(clover_kernel, "clover", [(144, LANES)], (clover[0],))
    received = exchanged(sends)
    psi, carried, *sends = call(
        functools.partial(middle_kernel, RELAXATION[0], True),
        "step0",
        [FIELD, CARRIED] + SENDS,
        (dilution, chosen, links, packed, carried, *received),
        total,
    )
    received = exchanged(sends)
    psi, carried, *sends = call(
        functools.partial(middle_kernel, RELAXATION[1], False),
        "step1",
        [FIELD, CARRIED] + SENDS,
        (dilution, chosen, links, packed, psi, carried, *received),
        total,
    )
    received = exchanged(sends)
    solutions, partial = call(
        functools.partial(last_kernel, RELAXATION[2]),
        "step2",
        [(24, 8, SITES), (64, 64)],
        (dilution, chosen, links, packed, eigvecs, psi, carried, *received),
        total,
    )
    parts = lax.all_to_all(partial, "space", 0, 0, tiled=True)
    volume = SITES * lax.axis_size("space")
    reduced = jnp.sum(parts, axis=0) * (1.0 / (3.0 * volume))
    return solutions.reshape(2, 4, 3, 1, 8, SITES), reduced.reshape(1, 1, 2, 4, 8)


def solution(mesh):
    in_specs = (
        P(),
        P(None, None, "tm", None, "space"),
        P("tm", None, None, None, None, "space"),
        P("tm", None, None, None, None, "space"),
    )
    out_specs = (P(None, None, None, "tm", None, "space"), P("tm", "space", None, None, None))
    return jax.shard_map(body, mesh=mesh, in_specs=in_specs, out_specs=out_specs, check_vma=False)
```

```python
import functools

import jax
import jax.numpy as jnp
from jax import lax
from jax.experimental import pallas as pl
from jax.experimental.pallas import tpu as pltpu
from jax.sharding import PartitionSpec as P

HOPPING = 0.125
RELAXATION = (0.9, 1.0, 1.1)
SITES = 216
LANES = 256
STRIDES = (36, 6, 1)
SPIN_BLOCKS = (
    ((0.0, -1j), (-1j, 0.0)),
    ((0.0, -1.0), (1.0, 0.0)),
    ((-1j, 0.0), (0.0, 1j)),
    ((1.0, 0.0), (0.0, 1.0)),
)
F32 = jnp.float32


def half(part, spin, colour):
    return (part * 2 + spin) * 3 + colour


def full(part, spin, colour):
    return (part * 4 + spin) * 3 + colour


def rotated(value, shift):
    shift %= LANES
    return value if shift == 0 else pltpu.roll(value, shift, axis=value.ndim - 1)


def add_turned(base, factor, real, imag):
    if factor == 1:
        return base[0] + real, base[1] + imag
    if factor == -1:
        return base[0] - real, base[1] - imag
    if factor == 1j:
        return base[0] - imag, base[1] + real
    return base[0] + imag, base[1] - real


def project(get, direction, parity):
    out = {}
    for spin in range(2):
        row = SPIN_BLOCKS[direction][spin]
        column = 0 if row[0] != 0 else 1
        factor = complex(parity * row[column])
        for colour in range(3):
            base = (get(0, spin, colour), get(1, spin, colour))
            real, imag = add_turned(base, factor, get(0, 2 + column, colour), get(1, 2 + column, colour))
            out[half(0, spin, colour)] = real
            out[half(1, spin, colour)] = imag
    return out


def turned(factor, real, imag):
    if factor == 1:
        return real, imag
    if factor == -1:
        return -real, -imag
    if factor == 1j:
        return -imag, real
    return imag, -real


def lower_of(direction, parity, spin):
    column = 0 if SPIN_BLOCKS[direction][0][spin] != 0 else 1
    return column, complex(parity * complex(SPIN_BLOCKS[direction][column][spin]).conjugate())


def rebuild(total, values, direction, parity):
    for spin in range(2):
        for colour in range(3):
            for part in range(2):
                q = full(part, spin, colour)
                total[q] = total[q] + values[half(part, spin, colour)]
    for spin in range(2):
        column, factor = lower_of(direction, parity, spin)
        for colour in range(3):
            q, r = full(0, 2 + spin, colour), full(1, 2 + spin, colour)
            total[q], total[r] = add_turned(
                (total[q], total[r]), factor, values[half(0, column, colour)], values[half(1, column, colour)]
            )


def rebuilt(values, direction, parity):
    out = {}
    for colour in range(3):
        for spin in range(2):
            for part in range(2):
                out[part, spin, colour] = values[half(part, spin, colour)]
            column, factor = lower_of(direction, parity, spin)
            out[0, 2 + spin, colour], out[1, 2 + spin, colour] = turned(
                factor, values[half(0, column, colour)], values[half(1, column, colour)]
            )
    return out


def link(links, direction, part, row, column):
    at = ((direction * 3 + row) * 3 + column) * 2 + part
    return jnp.broadcast_to(links[at : at + 1, :], (8, LANES))


def color_times(links, direction, values, adjoint):
    out = {}
    for row in range(3):
        for spin in range(2):
            real = imag = None
            for column in range(3):
                at = (column, row) if adjoint else (row, column)
                u_real = link(links, direction, 0, *at)
                u_imag = link(links, direction, 1, *at)
                v_real, v_imag = values[half(0, spin, column)], values[half(1, spin, column)]
                if adjoint:
                    a = u_real * v_real + u_imag * v_imag
                    b = u_real * v_imag - u_imag * v_real
                else:
                    a = u_real * v_real - u_imag * v_imag
                    b = u_real * v_imag + u_imag * v_real
                real = a if real is None else real + a
                imag = b if imag is None else imag + b
            out[half(0, spin, row)] = real
            out[half(1, spin, row)] = imag
    return out


def lane_slots():
    lane = lax.broadcasted_iota(jnp.int32, (8, LANES), 1)
    sixth = lane * 10923 >> 16
    x = sixth * 10923 >> 16
    return x, sixth - 6 * x, lane - 6 * sixth


def even_bits(dimension):
    bits = lax.axis_index("space") >> 2 * (2 - dimension)
    return ((bits ^ bits >> 1) & 1) == 0


def column_of(row):
    square = (8, 8)
    same = lax.broadcasted_iota(jnp.int32, square, 0) == lax.broadcasted_iota(jnp.int32, square, 1)
    return jnp.sum(jnp.where(same, jnp.broadcast_to(row.astype(F32), square), 0.0), axis=1, keepdims=True)


def place(sends, direction, vector, first, second):
    if direction == 0:
        number = lax.axis_index("space") >> 4
        sends[0][number ^ 1, vector] = first
        sends[0][number ^ 2, vector] = second
    else:
        sends[2 * direction - 1][vector] = first
        sends[2 * direction][vector] = second


def arrived(received, direction, vector):
    if direction == 0:
        number = lax.axis_index("space") >> 4
        first, second = received[0][number ^ 1, vector], received[0][number ^ 2, vector]
    else:
        first, second = received[2 * direction - 1][vector], received[2 * direction][vector]
    low_is_ahead = even_bits(direction)
    return jnp.where(low_is_ahead, first, second), jnp.where(low_is_ahead, second, first)


def packed_low(values, slot, stride):
    out = values[0]
    for r in range(1, 6):
        out = jnp.where(slot == r, rotated(values[r], stride * r), out)
    return out


def packed_high(values, slot, stride):
    out = rotated(values[0], -5 * stride)
    for r in range(1, 6):
        out = jnp.where(slot == r, rotated(values[r], stride * (r - 5)), out)
    return out


def emit_faces(get, carried, sends):
    slots = lane_slots()
    for direction in range(3):
        stride, slot = STRIDES[direction], slots[direction]
        low_is_ahead = even_bits(direction)
        forward = project(get, direction, -1)
        for vector in range(2):
            own = range(6 * vector, 6 * vector + 6)
            low = packed_low([forward[q] for q in own], slot, stride)
            high = packed_high([carried[direction * 12 + q] for q in own], slot, stride)
            place(sends, direction, vector, jnp.where(low_is_ahead, high, low), jnp.where(low_is_ahead, low, high))


def emit_slices(get, links, slices):
    forward = project(get, 3, -1)
    backward = color_times(links, 3, project(get, 3, 1), True)
    for q in range(12):
        slices[0][q] = forward[q]
        slices[1][q] = backward[q]


def carry(get, links, carried):
    for direction in range(3):
        backward = color_times(links, direction, project(get, direction, 1), True)
        for q in range(12):
            carried[direction * 12 + q] = backward[q]


def pick_of(dilution):
    number = jnp.broadcast_to(column_of(dilution[0:1, :]), (8, 64)).astype(jnp.int32)
    return (lax.broadcasted_iota(jnp.int32, (8, 64), 1) == number).astype(F32)


def product(left, right, contracted):
    return lax.dot_general(
        left,
        right,
        ((contracted[:1], contracted[1:]), ((), ())),
        precision=lax.Precision.HIGHEST,
        preferred_element_type=F32,
    )


def masks_of(dilution):
    spins = jnp.broadcast_to(column_of(dilution[1:2, :]), (8, LANES))
    return [(spins == spin).astype(F32) for spin in range(4)]


def source_getter(chosen, masks):
    return lambda part, spin, colour: masks[spin] * chosen[part * 3 + colour]


def start_kernel(dilution, eigvecs, gauge, chosen, links, carried, *rest):
    sends, slices, later, basis = rest[:5], rest[5:7], rest[7], rest[8]
    links[...] = jnp.zeros_like(links)
    for direction in range(4):
        for row in range(3):
            for column in range(3):
                at = ((direction * 3 + row) * 3 + column) * 2
                links[at : at + 2, 0:SITES] = gauge[direction, row, column]
    pick = pick_of(dilution)
    basis[...] = jnp.zeros_like(basis)
    for part in range(2):
        for colour in range(3):
            basis[part * 3 + colour, :, 0:SITES] = eigvecs[part, colour]
    for q in range(6):
        chosen[q] = product(pick, basis[q], (1, 0))
    slots = lane_slots()
    sends[0][...] = jnp.zeros_like(sends[0])
    for direction in range(4):
        for group in range(-1, 8 if direction < 3 else 0):
            plain = [chosen[q] if group < 0 else basis[q, 8 * group : 8 * group + 8, :] for q in range(6)]
            times = []
            for part in range(2):
                for row in range(3):
                    total = None
                    for column in range(3):
                        u_real = link(links, direction, 0, column, row)
                        u_imag = link(links, direction, 1, column, row)
                        real, imag = plain[column], plain[3 + column]
                        term = u_real * real + u_imag * imag if part == 0 else u_real * imag - u_imag * real
                        total = term if total is None else total + term
                    times.append(total)
            if direction == 3:
                for q in range(6):
                    slices[0][q] = plain[q]
                    slices[1][q] = times[q]
                continue
            stride, slot = STRIDES[direction], slots[direction]
            low_is_ahead = even_bits(direction)
            low = packed_low(plain, slot, stride)
            high = packed_high(times, slot, stride)
            first, second = jnp.where(low_is_ahead, high, low), jnp.where(low_is_ahead, low, high)
            if group < 4:
                place(sends, direction, 1 + group, first, second)
            else:
                later[2 * direction, group - 4] = first
                later[2 * direction + 1, group - 4] = second
    carry(source_getter(chosen, masks_of(dilution)), links, carried)


def clover_kernel(clover, packed):
    packed[...] = jnp.zeros_like(packed)
    for part in range(2):
        for row in range(6):
            for column in range(6):
                at = ((part * 6 + row) * 6 + column) * 2
                packed[at : at + 2, 0:SITES] = clover[part, row, column]


def hop(total, links, get, carried, halos):
    total[...] = jnp.zeros_like(total)
    slots = lane_slots()
    for direction in range(3):
        stride, slot = STRIDES[direction], slots[direction]
        ahead, behind = halos[direction]
        if get is None and ahead is None:
            continue
        forward, backward = {}, {}
        if get is not None:
            for q, value in project(get, direction, -1).items():
                forward[q] = rotated(value, -stride)
                backward[q] = rotated(carried[direction * 12 + q], stride)
        for q in range(12):
            forward[q] = jnp.where(
                slot == 5, 0.0 if ahead is None else ahead[q], 0.0 if get is None else forward[q]
            )
            backward[q] = jnp.where(
                slot == 0, 0.0 if behind is None else behind[q], 0.0 if get is None else backward[q]
            )
        rebuild(total, color_times(links, direction, forward, False), direction, -1)
        rebuild(total, backward, direction, 1)
    ahead, behind = halos[3]
    if ahead is not None:
        rebuild(total, color_times(links, 3, ahead, False), 3, -1)
        rebuild(total, behind, 3, 1)


def slice_halos(slices):
    return [(None, None)] * 3 + [(slices[0], slices[1])]


def field_halos(received):
    halos = []
    for direction in range(3):
        stride = STRIDES[direction]
        ahead, behind = {}, {}
        for vector in range(2):
            from_ahead, from_behind = arrived(received, direction, vector)
            for r in range(6):
                ahead[6 * vector + r] = rotated(from_ahead, stride * (5 - r))
                behind[6 * vector + r] = rotated(from_behind, -stride * r)
        halos.append((ahead, behind))
    return halos


def basis_face(first, second, direction):
    both = [arrived(first, direction, 1 + group) for group in range(4)]
    both += [arrived(second, direction, 2 + group) for group in range(4)]
    return tuple(jnp.concatenate([pair[side] for pair in both], axis=0) for side in range(2))


def source_halos(received, slices, masks):
    halos = []
    for direction in range(4):
        if direction < 3:
            stride = STRIDES[direction]
            from_ahead, from_behind = arrived(received, direction, 0)
            ahead = [rotated(from_ahead, stride * (5 - r)) for r in range(6)]
            behind = [rotated(from_behind, -stride * r) for r in range(6)]
        else:
            ahead, behind = slices
        halos.append(
            (
                project(source_getter(ahead, masks), direction, -1),
                project(source_getter(behind, masks), direction, 1),
            )
        )
    return halos


def relax(weight, get, source, clover, total, store):
    for chiral in range(2):
        for row in range(6):
            real = imag = None
            for column in range(6):
                at = (row * 6 + column) * 2 + chiral
                a_real = jnp.broadcast_to(clover[at : at + 1, :], (8, LANES))
                a_imag = jnp.broadcast_to(clover[72 + at : 73 + at, :], (8, LANES))
                spin, colour = 2 * chiral + column // 3, column % 3
                v_real, v_imag = get(0, spin, colour), get(1, spin, colour)
                a = a_real * v_real - a_imag * v_imag
                b = a_real * v_imag + a_imag * v_real
                real = a if real is None else real + a
                imag = b if imag is None else imag + b
            spin, colour = 2 * chiral + row // 3, row % 3
            for part, applied in ((0, real), (1, imag)):
                q = full(part, spin, colour)
                store[q] = get(part, spin, colour) + weight * (
                    source(part, spin, colour) - (applied - HOPPING * total[q])
                )


def getter(ref):
    return lambda part, spin, colour: ref[full(part, spin, colour)]


def first_kernel(dilution, chosen, links, clover, carried_in, later, *rest):
    received, slices, psi, carried = rest[:5], rest[5:7], rest[7], rest[8]
    sends, next_slices, total = rest[9:14], rest[14:16], rest[16]
    masks = masks_of(dilution)
    source = source_getter(chosen, masks)
    hop(total, links, source, carried_in, source_halos(received, slices, masks))
    relax(RELAXATION[0], source, source, clover, total, psi)
    sends[0][...] = jnp.zeros_like(sends[0])
    carry(getter(psi), links, carried)
    emit_faces(getter(psi), carried, sends)
    for direction in range(3):
        for group in range(4):
            place(sends, direction, 2 + group, later[2 * direction, group], later[2 * direction + 1, group])
    emit_slices(getter(psi), links, next_slices)


def projected_rows(values, place_at):
    rows = []
    for part in range(2):
        for spin in range(4):
            real = [values(part, spin, colour) for colour in range(3)]
            other = [values(1 - part, spin, colour) for colour in range(3)]
            if part == 1:
                other = [-value for value in other]
            rows.append(place_at(real, other))
    return rows


def projections(eigvecs, inner, psi, carried, first, second):
    summed = None
    rows = projected_rows(getter(inner), lambda real, other: real + other)
    for part in range(2):
        for colour in range(3):
            field = jnp.concatenate([row[3 * part + colour][:, 0:SITES] for row in rows], axis=0)
            term = product(eigvecs[part, colour], field, (1, 1))
            summed = term if summed is None else summed + term
    slots = lane_slots()
    inside = lax.broadcasted_iota(jnp.int32, (8, LANES), 1) < SITES
    faces = None
    for direction in range(3):
        stride, slot = STRIDES[direction], slots[direction]
        low = rebuilt(project(getter(psi), direction, -1), direction, -1)
        high = rebuilt([carried[direction * 12 + q] for q in range(12)], direction, 1)
        from_ahead, from_behind = basis_face(first, second, direction)
        for values, face, pack in ((low, from_behind, packed_low), (high, from_ahead, packed_high)):
            rows = projected_rows(
                lambda part, spin, colour: values[part, spin, colour],
                lambda real, other: jnp.where(inside, pack(real + other, slot, stride), 0.0),
            )
            term = product(face, jnp.concatenate(rows, axis=0), (1, 1))
            faces = term if faces is None else faces + term
    return summed + (RELAXATION[2] * HOPPING) * faces


def second_kernel(dilution, chosen, links, clover, spinor, carried_in, *rest):
    received, slices, (psi, carried, inner), next_slices, total = rest[:5], rest[5:7], rest[7:10], rest[10:12], rest[12]
    source = source_getter(chosen, masks_of(dilution))
    hop(total, links, getter(spinor), carried_in, field_halos(received) + [(slices[0], slices[1])])
    relax(RELAXATION[1], getter(spinor), source, clover, total, psi)
    emit_slices(getter(psi), links, next_slices)
    carry(getter(psi), links, carried)
    hop(total, links, getter(psi), carried, [(None, None)] * 4)
    relax(RELAXATION[2], getter(psi), source, clover, total, inner)


def project_kernel(links, eigvecs, psi, carried, inner_in, *rest):
    slices, first, second, inner, sends, total = rest[:2], rest[2:7], rest[7:12], rest[12], rest[13:18], rest[18]
    hop(total, links, None, None, slice_halos(slices))
    for q in range(24):
        inner[q] = inner_in[q] + (RELAXATION[2] * HOPPING) * total[q]
    sends[0][...] = jnp.zeros_like(sends[0])
    emit_faces(getter(psi), carried, sends)
    partial = projections(eigvecs, inner, psi, carried, first, second)
    for number in range(4):
        at = 16 * number
        sends[0][number, 2, :, 0:64] = partial[at : at + 8, :]
        sends[0][number, 2, :, 128:192] = partial[at + 8 : at + 16, :]


def line_sum_kernel(received, *rest):
    out = rest[-1]
    summed = received[0, 2]
    for number in range(1, 4):
        summed = summed + received[number, 2]
    out[0:8, :] = summed[:, 0:64]
    out[8:16, :] = summed[:, 128:192]


def last_kernel(links, inner, *rest):
    received, solutions, total = rest[:5], rest[5], rest[6]
    hop(total, links, None, None, field_halos(received) + [(None, None)])
    for q in range(24):
        solutions[q] = (inner[q] + (RELAXATION[2] * HOPPING) * total[q])[:, 0:SITES]


def call(kernel, name, outs, args, scratch=()):
    vmem = pl.BlockSpec(memory_space=pltpu.VMEM)
    return pl.pallas_call(
        kernel,
        name=name,
        out_shape=[jax.ShapeDtypeStruct(shape, F32) for shape in outs],
        in_specs=[vmem] * len(args),
        out_specs=[vmem] * len(outs),
        scratch_shapes=[pltpu.VMEM(shape, F32) for shape in scratch],
        compiler_params=pltpu.CompilerParams(vmem_limit_bytes=16 << 20),
    )(*args)


SLICES = [(12, 8, LANES)] * 2
FIELD = (24, 8, LANES)
CARRIED = (36, 8, LANES)


def faces_of(vectors):
    return [(4, vectors, 8, LANES)] + [(vectors, 8, LANES)] * 4


BITS = (None, 2, 3, 0, 1)
ORDER = (2, 1, 4, 3)


def exchanged(sends):
    size = lax.axis_size("space")
    received = [None] * 5
    lines = [[i + 16 * n for n in range(4)] for i in range(16)]
    received[0] = lax.all_to_all(sends[0], "space", 0, 0, axis_index_groups=lines, tiled=True)
    for n in ORDER:
        flip = [(i, i ^ 1 << BITS[n]) for i in range(size)]
        received[n] = lax.ppermute(sends[n], "space", flip)
    return received


def shifted(slices):
    length = lax.axis_size("tm")
    return [
        lax.ppermute(slices[0], "tm", [(i, (i - 1) % length) for i in range(length)]),
        lax.ppermute(slices[1], "tm", [(i, (i + 1) % length) for i in range(length)]),
    ]


def body(dilution, eigvecs, gauge_links, clover):
    eigvecs = eigvecs[:, :, 0]
    dilution = dilution.T
    gauge_links = gauge_links.transpose(0, 1, 3, 4, 2, 5)
    clover = clover.transpose(0, 1, 3, 4, 2, 5)
    chosen, links, carried, *sends, ahead, behind, later = call(
        start_kernel,
        "start",
        [(6, 8, LANES), (72, LANES), CARRIED] + faces_of(5) + [(6, 8, LANES)] * 2 + [(6, 4, 8, LANES)],
        (dilution, eigvecs, gauge_links[0]),
        [(6, 64, LANES)],
    )
    (packed,) = call(clover_kernel, "clover", [(144, LANES)], (clover[0],))
    first = exchanged(sends)
    slices = shifted((ahead, behind))
    psi, carried, *sends, ahead, behind = call(
        first_kernel,
        "step0",
        [FIELD, CARRIED] + faces_of(6) + SLICES,
        (dilution, chosen, links, packed, carried, later, *first, *slices),
        [FIELD],
    )
    second = exchanged(sends)
    slices = shifted((ahead, behind))
    psi, carried, inner, ahead, behind = call(
        second_kernel,
        "step1",
        [FIELD, CARRIED, FIELD] + SLICES,
        (dilution, chosen, links, packed, psi, carried, *second, *slices),
        [FIELD],
    )
    slices = shifted((ahead, behind))
    inner, *sends = call(
        project_kernel,
        "project",
        [FIELD] + faces_of(3)[:1] + faces_of(2)[1:],
        (links, eigvecs, psi, carried, inner, *slices, *first, *second),
        [FIELD],
    )
    third = exchanged(sends)
    (rows,) = call(line_sum_kernel, "line_sum", [(16, 64)], third)
    blocks = [[16 * n + i for i in range(16)] for n in range(4)]
    parts = lax.all_to_all(rows, "space", 0, 0, axis_index_groups=blocks, tiled=True)
    volume = SITES * lax.axis_size("space")
    reduced = jnp.sum(parts, axis=0) * (1.0 / (3.0 * volume))
    (solutions,) = call(last_kernel, "step2", [(24, 8, SITES)], (links, inner, *third), [FIELD])
    return solutions.reshape(2, 4, 3, 1, 8, SITES), reduced.reshape(1, 1, 2, 4, 8)


def solution(mesh):
    in_specs = (
        P(),
        P(None, None, "tm", None, "space"),
        P("tm", None, None, None, None, "space"),
        P("tm", None, None, None, None, "space"),
    )
    out_specs = (P(None, None, None, "tm", None, "space"), P("tm", "space", None, None, None))
    return jax.shard_map(body, mesh=mesh, in_specs=in_specs, out_specs=out_specs, check_vma=False)
```

```python
import jax
import jax.numpy as jnp
from jax import lax
from jax.experimental import pallas as pl
from jax.experimental.pallas import tpu as pltpu
from jax.sharding import PartitionSpec as P

HOPPING = 0.125
RELAXATION = (0.9, 1.0, 1.1)
SITES = 216
LANES = 256
STRIDES = (36, 6, 1)
SPIN_BLOCKS = (
    ((0.0, -1j), (-1j, 0.0)),
    ((0.0, -1.0), (1.0, 0.0)),
    ((-1j, 0.0), (0.0, 1j)),
    ((1.0, 0.0), (0.0, 1.0)),
)
F32 = jnp.float32


def half(part, spin, colour):
    return (part * 2 + spin) * 3 + colour


def full(part, spin, colour):
    return (part * 4 + spin) * 3 + colour


def rotated(value, shift):
    shift %= LANES
    return value if shift == 0 else pltpu.roll(value, shift, axis=value.ndim - 1)


def add_turned(base, factor, real, imag):
    if factor == 1:
        return base[0] + real, base[1] + imag
    if factor == -1:
        return base[0] - real, base[1] - imag
    if factor == 1j:
        return base[0] - imag, base[1] + real
    return base[0] + imag, base[1] - real


def project(get, direction, parity):
    out = {}
    for spin in range(2):
        row = SPIN_BLOCKS[direction][spin]
        column = 0 if row[0] != 0 else 1
        factor = complex(parity * row[column])
        for colour in range(3):
            base = (get(0, spin, colour), get(1, spin, colour))
            real, imag = add_turned(base, factor, get(0, 2 + column, colour), get(1, 2 + column, colour))
            out[half(0, spin, colour)] = real
            out[half(1, spin, colour)] = imag
    return out


def turned(factor, real, imag):
    if factor == 1:
        return real, imag
    if factor == -1:
        return -real, -imag
    if factor == 1j:
        return -imag, real
    return imag, -real


def lower_of(direction, parity, spin):
    column = 0 if SPIN_BLOCKS[direction][0][spin] != 0 else 1
    return column, complex(parity * complex(SPIN_BLOCKS[direction][column][spin]).conjugate())


def rebuild(total, values, direction, parity):
    for spin in range(2):
        for colour in range(3):
            for part in range(2):
                q = full(part, spin, colour)
                total[q] = total[q] + values[half(part, spin, colour)]
    for spin in range(2):
        column, factor = lower_of(direction, parity, spin)
        for colour in range(3):
            q, r = full(0, 2 + spin, colour), full(1, 2 + spin, colour)
            total[q], total[r] = add_turned(
                (total[q], total[r]), factor, values[half(0, column, colour)], values[half(1, column, colour)]
            )


def rebuilt(values, direction, parity):
    out = {}
    for colour in range(3):
        for spin in range(2):
            for part in range(2):
                out[part, spin, colour] = values[half(part, spin, colour)]
            column, factor = lower_of(direction, parity, spin)
            out[0, 2 + spin, colour], out[1, 2 + spin, colour] = turned(
                factor, values[half(0, column, colour)], values[half(1, column, colour)]
            )
    return out


def link(links, direction, part, row, column):
    at = ((direction * 3 + row) * 3 + column) * 2 + part
    return jnp.broadcast_to(links[at : at + 1, :], (8, LANES))


def color_times(links, direction, values, adjoint):
    out = {}
    for row in range(3):
        for spin in range(2):
            real = imag = None
            for column in range(3):
                at = (column, row) if adjoint else (row, column)
                u_real = link(links, direction, 0, *at)
                u_imag = link(links, direction, 1, *at)
                v_real, v_imag = values[half(0, spin, column)], values[half(1, spin, column)]
                if adjoint:
                    a = u_real * v_real + u_imag * v_imag
                    b = u_real * v_imag - u_imag * v_real
                else:
                    a = u_real * v_real - u_imag * v_imag
                    b = u_real * v_imag + u_imag * v_real
                real = a if real is None else real + a
                imag = b if imag is None else imag + b
            out[half(0, spin, row)] = real
            out[half(1, spin, row)] = imag
    return out


def lane_slots():
    lane = lax.broadcasted_iota(jnp.int32, (8, LANES), 1)
    sixth = lane * 10923 >> 16
    x = sixth * 10923 >> 16
    return x, sixth - 6 * x, lane - 6 * sixth


def even_bits(dimension):
    bits = lax.axis_index("space") >> 2 * (2 - dimension)
    return ((bits ^ bits >> 1) & 1) == 0


def column_of(row):
    square = (8, 8)
    same = lax.broadcasted_iota(jnp.int32, square, 0) == lax.broadcasted_iota(jnp.int32, square, 1)
    return jnp.sum(jnp.where(same, jnp.broadcast_to(row.astype(F32), square), 0.0), axis=1, keepdims=True)


def place(sends, direction, vector, first, second):
    if direction == 0 and len(sends) == 5:
        number = lax.axis_index("space") >> 4
        sends[0][number ^ 1, vector] = first
        sends[0][number ^ 2, vector] = second
    else:
        sends[2 * direction - 6][vector] = first
        sends[2 * direction - 5][vector] = second


def arrived(received, direction, vector):
    if direction == 0 and len(received) == 5:
        number = lax.axis_index("space") >> 4
        first, second = received[0][number ^ 1, vector], received[0][number ^ 2, vector]
    else:
        first, second = received[2 * direction - 6][vector], received[2 * direction - 5][vector]
    low_is_ahead = even_bits(direction)
    return jnp.where(low_is_ahead, first, second), jnp.where(low_is_ahead, second, first)


def packed_low(values, slot, stride):
    out = values[0]
    for r in range(1, 6):
        out = jnp.where(slot == r, rotated(values[r], stride * r), out)
    return out


def packed_high(values, slot, stride):
    out = rotated(values[0], -5 * stride)
    for r in range(1, 6):
        out = jnp.where(slot == r, rotated(values[r], stride * (r - 5)), out)
    return out


def emit_faces(get, carried, sends):
    slots = lane_slots()
    for direction in range(3):
        stride, slot = STRIDES[direction], slots[direction]
        low_is_ahead = even_bits(direction)
        forward = project(get, direction, -1)
        for vector in range(2):
            own = range(6 * vector, 6 * vector + 6)
            low = packed_low([forward[q] for q in own], slot, stride)
            high = packed_high([carried[direction * 12 + q] for q in own], slot, stride)
            place(sends, direction, vector, jnp.where(low_is_ahead, high, low), jnp.where(low_is_ahead, low, high))


def emit_slices(get, links, slices):
    forward = project(get, 3, -1)
    backward = color_times(links, 3, project(get, 3, 1), True)
    for q in range(12):
        slices[0][q] = forward[q]
        slices[1][q] = backward[q]


def carry(get, links, carried):
    for direction in range(3):
        backward = color_times(links, direction, project(get, direction, 1), True)
        for q in range(12):
            carried[direction * 12 + q] = backward[q]


def pick_of(dilution):
    number = jnp.broadcast_to(column_of(dilution[0:1, :]), (8, 64)).astype(jnp.int32)
    return (lax.broadcasted_iota(jnp.int32, (8, 64), 1) == number).astype(F32)


def product(left, right, contracted):
    return lax.dot_general(
        left,
        right,
        ((contracted[:1], contracted[1:]), ((), ())),
        precision=lax.Precision.HIGHEST,
        preferred_element_type=F32,
    )


def masks_of(dilution):
    spins = jnp.broadcast_to(column_of(dilution[1:2, :]), (8, LANES))
    return [(spins == spin).astype(F32) for spin in range(4)]


def source_getter(chosen, masks):
    return lambda part, spin, colour: masks[spin] * chosen[part * 3 + colour]


def start_kernel(dilution, eigvecs, gauge, chosen, links, carried, *rest):
    sends, slices, later, basis = rest[:6], rest[6:8], rest[8], rest[9]
    held, copied = rest[10:13], rest[13]
    copies = [
        pltpu.make_async_copy(source, target, copied.at[n])
        for n, (source, target) in enumerate(zip((dilution, eigvecs, gauge), held))
    ]
    for copy in reversed(copies):
        copy.start()
    links[...] = jnp.zeros_like(links)
    basis[...] = jnp.zeros_like(basis)
    for copy in copies:
        copy.wait()
    dilution, eigvecs, gauge = held
    for direction in range(4):
        for row in range(3):
            for column in range(3):
                at = ((direction * 3 + row) * 3 + column) * 2
                links[at : at + 2, 0:SITES] = gauge[direction, row, column]
    pick = pick_of(dilution)
    for part in range(2):
        for colour in range(3):
            basis[part * 3 + colour, :, 0:SITES] = eigvecs[part, colour]
    for q in range(6):
        chosen[q] = product(pick, basis[q], (1, 0))
    slots = lane_slots()
    for direction in range(4):
        for group in range(-1, 8 if direction < 3 else 0):
            plain = [chosen[q] if group < 0 else basis[q, 8 * group : 8 * group + 8, :] for q in range(6)]
            times = []
            for part in range(2):
                for row in range(3):
                    total = None
                    for column in range(3):
                        u_real = link(links, direction, 0, column, row)
                        u_imag = link(links, direction, 1, column, row)
                        real, imag = plain[column], plain[3 + column]
                        term = u_real * real + u_imag * imag if part == 0 else u_real * imag - u_imag * real
                        total = term if total is None else total + term
                    times.append(total)
            if direction == 3:
                for q in range(6):
                    slices[0][q] = plain[q]
                    slices[1][q] = times[q]
                continue
            stride, slot = STRIDES[direction], slots[direction]
            low_is_ahead = even_bits(direction)
            low = packed_low(plain, slot, stride)
            high = packed_high(times, slot, stride)
            first, second = jnp.where(low_is_ahead, high, low), jnp.where(low_is_ahead, low, high)
            if group < 4:
                place(sends, direction, 1 + group, first, second)
            else:
                later[2 * direction, group - 4] = first
                later[2 * direction + 1, group - 4] = second
    carry(source_getter(chosen, masks_of(dilution)), links, carried)


def clover_kernel(clover, packed):
    packed[...] = jnp.zeros_like(packed)
    for part in range(2):
        for row in range(6):
            for column in range(6):
                at = ((part * 6 + row) * 6 + column) * 2
                packed[at : at + 2, 0:SITES] = clover[part, row, column]


def hop(total, links, get, carried, halos):
    total[...] = jnp.zeros_like(total)
    slots = lane_slots()
    for direction in range(3):
        stride, slot = STRIDES[direction], slots[direction]
        ahead, behind = halos[direction]
        if get is None and ahead is None:
            continue
        forward, backward = {}, {}
        if get is not None:
            for q, value in project(get, direction, -1).items():
                forward[q] = rotated(value, -stride)
                backward[q] = rotated(carried[direction * 12 + q], stride)
        for q in range(12):
            forward[q] = jnp.where(
                slot == 5, 0.0 if ahead is None else ahead[q], 0.0 if get is None else forward[q]
            )
            backward[q] = jnp.where(
                slot == 0, 0.0 if behind is None else behind[q], 0.0 if get is None else backward[q]
            )
        rebuild(total, color_times(links, direction, forward, False), direction, -1)
        rebuild(total, backward, direction, 1)
    ahead, behind = halos[3]
    if ahead is not None:
        rebuild(total, color_times(links, 3, ahead, False), 3, -1)
        rebuild(total, behind, 3, 1)


def slice_halos(slices):
    return [(None, None)] * 3 + [(slices[0], slices[1])]


def field_halos(received):
    halos = []
    for direction in range(3):
        stride = STRIDES[direction]
        ahead, behind = {}, {}
        for vector in range(2):
            from_ahead, from_behind = arrived(received, direction, vector)
            for r in range(6):
                ahead[6 * vector + r] = rotated(from_ahead, stride * (5 - r))
                behind[6 * vector + r] = rotated(from_behind, -stride * r)
        halos.append((ahead, behind))
    return halos


def basis_face(first, second, direction):
    both = [arrived(first, direction, 1 + group) for group in range(4)]
    both += [arrived(second, direction, 2 + group) for group in range(4)]
    return tuple(jnp.concatenate([pair[side] for pair in both], axis=0) for side in range(2))


def source_halos(received, slices, masks):
    halos = []
    for direction in range(4):
        if direction < 3:
            stride = STRIDES[direction]
            from_ahead, from_behind = arrived(received, direction, 0)
            ahead = [rotated(from_ahead, stride * (5 - r)) for r in range(6)]
            behind = [rotated(from_behind, -stride * r) for r in range(6)]
        else:
            ahead, behind = slices
        halos.append(
            (
                project(source_getter(ahead, masks), direction, -1),
                project(source_getter(behind, masks), direction, 1),
            )
        )
    return halos


def relax(weight, get, source, clover, total, store):
    for chiral in range(2):
        for row in range(6):
            real = imag = None
            for column in range(6):
                at = (row * 6 + column) * 2 + chiral
                a_real = jnp.broadcast_to(clover[at : at + 1, :], (8, LANES))
                a_imag = jnp.broadcast_to(clover[72 + at : 73 + at, :], (8, LANES))
                spin, colour = 2 * chiral + column // 3, column % 3
                v_real, v_imag = get(0, spin, colour), get(1, spin, colour)
                a = a_real * v_real - a_imag * v_imag
                b = a_real * v_imag + a_imag * v_real
                real = a if real is None else real + a
                imag = b if imag is None else imag + b
            spin, colour = 2 * chiral + row // 3, row % 3
            for part, applied in ((0, real), (1, imag)):
                q = full(part, spin, colour)
                store[q] = get(part, spin, colour) + weight * (
                    source(part, spin, colour) - (applied - HOPPING * total[q])
                )


def getter(ref):
    return lambda part, spin, colour: ref[full(part, spin, colour)]


def first_kernel(dilution, chosen, links, clover, carried_in, later, *rest):
    received, slices, psi, carried = rest[:6], rest[6:8], rest[8], rest[9]
    sends, next_slices, total = rest[10:16], rest[16:18], rest[18]
    masks = masks_of(dilution)
    source = source_getter(chosen, masks)
    hop(total, links, source, carried_in, source_halos(received, slices, masks))
    relax(RELAXATION[0], source, source, clover, total, psi)
    carry(getter(psi), links, carried)
    emit_faces(getter(psi), carried, sends)
    for direction in range(3):
        for group in range(4):
            place(sends, direction, 2 + group, later[2 * direction, group], later[2 * direction + 1, group])
    emit_slices(getter(psi), links, next_slices)


def projected_rows(values, place_at):
    rows = []
    for part in range(2):
        for spin in range(4):
            real = [values(part, spin, colour) for colour in range(3)]
            other = [values(1 - part, spin, colour) for colour in range(3)]
            if part == 1:
                other = [-value for value in other]
            rows.append(place_at(real, other))
    return rows


def projections(eigvecs, inner, psi, carried, first, second):
    summed = None
    rows = projected_rows(getter(inner), lambda real, other: real + other)
    for part in range(2):
        for colour in range(3):
            field = jnp.concatenate([row[3 * part + colour][:, 0:SITES] for row in rows], axis=0)
            term = product(eigvecs[part, colour], field, (1, 1))
            summed = term if summed is None else summed + term
    slots = lane_slots()
    inside = lax.broadcasted_iota(jnp.int32, (8, LANES), 1) < SITES
    faces = None
    for direction in range(3):
        stride, slot = STRIDES[direction], slots[direction]
        low = rebuilt(project(getter(psi), direction, -1), direction, -1)
        high = rebuilt([carried[direction * 12 + q] for q in range(12)], direction, 1)
        from_ahead, from_behind = basis_face(first, second, direction)
        for values, face, pack in ((low, from_behind, packed_low), (high, from_ahead, packed_high)):
            rows = projected_rows(
                lambda part, spin, colour: values[part, spin, colour],
                lambda real, other: jnp.where(inside, pack(real + other, slot, stride), 0.0),
            )
            term = product(face, jnp.concatenate(rows, axis=0), (1, 1))
            faces = term if faces is None else faces + term
    return summed + (RELAXATION[2] * HOPPING) * faces


def second_kernel(dilution, chosen, links, clover, spinor, carried_in, *rest):
    received, slices, (psi, carried, inner), next_slices, total = rest[:6], rest[6:8], rest[8:11], rest[11:13], rest[13]
    source = source_getter(chosen, masks_of(dilution))
    hop(total, links, getter(spinor), carried_in, field_halos(received) + [(slices[0], slices[1])])
    relax(RELAXATION[1], getter(spinor), source, clover, total, psi)
    emit_slices(getter(psi), links, next_slices)
    carry(getter(psi), links, carried)
    hop(total, links, getter(psi), carried, [(None, None)] * 4)
    relax(RELAXATION[2], getter(psi), source, clover, total, inner)


def project_kernel(links, eigvecs, psi, carried, inner_in, *rest):
    slices, first, second, inner, sends, total = rest[:2], rest[2:8], rest[8:14], rest[14], rest[15:20], rest[20]
    hop(total, links, None, None, slice_halos(slices))
    for q in range(24):
        inner[q] = inner_in[q] + (RELAXATION[2] * HOPPING) * total[q]
    sends[0][...] = jnp.zeros_like(sends[0])
    emit_faces(getter(psi), carried, sends)
    partial = projections(eigvecs, inner, psi, carried, first, second)
    for number in range(4):
        at = 16 * number
        sends[0][number, 2, :, 0:64] = partial[at : at + 8, :]
        sends[0][number, 2, :, 128:192] = partial[at + 8 : at + 16, :]


def line_sum_kernel(received, *rest):
    out = rest[-1]
    summed = received[0, 2]
    for number in range(1, 4):
        summed = summed + received[number, 2]
    out[0:8, :] = summed[:, 0:64]
    out[8:16, :] = summed[:, 128:192]


def last_kernel(links, inner, *rest):
    received, solutions, total = rest[:5], rest[5], rest[6]
    hop(total, links, None, None, field_halos(received) + [(None, None)])
    for q in range(24):
        solutions[q] = (inner[q] + (RELAXATION[2] * HOPPING) * total[q])[:, 0:SITES]


def call(kernel, outs, args, scratch=(), place=pltpu.VMEM):
    vmem = pl.BlockSpec(memory_space=pltpu.VMEM)
    return pl.pallas_call(
        kernel,
        out_shape=[jax.ShapeDtypeStruct(shape, F32) for shape in outs],
        in_specs=[pl.BlockSpec(memory_space=place)] * len(args),
        out_specs=[vmem] * len(outs),
        scratch_shapes=[pltpu.VMEM(shape, F32) if isinstance(shape, tuple) else shape for shape in scratch],
        compiler_params=pltpu.CompilerParams(vmem_limit_bytes=16 << 20),
    )(*args)


SLICES = [(12, 8, LANES)] * 2
FIELD = (24, 8, LANES)
CARRIED = (36, 8, LANES)


def faces_of(vectors):
    return [(vectors, 8, LANES)] * 6


BITS = (4, 5, 2, 3, 0, 1)


def flipped(value, n):
    return lax.ppermute(value, "space", [(i, i ^ 1 << BITS[n]) for i in range(lax.axis_size("space"))])


def on_line(value):
    lines = [[i + 16 * n for n in range(4)] for i in range(16)]
    return lax.all_to_all(value, "space", 0, 0, axis_index_groups=lines, tiled=True)


def shifted(slices):
    length = lax.axis_size("tm")
    out = []
    for n, by in enumerate((-1, 1)):
        out.append(lax.ppermute(slices[n], "tm", [(i, (i + by) % length) for i in range(length)]))
    return out


def exchanged(sends, slices):
    return [flipped(send, n) for n, send in enumerate(sends)], shifted(slices)


def body(dilution, eigvecs, gauge_links, clover):
    eigvecs = eigvecs[:, :, 0]
    dilution = dilution.T
    gauge_links = gauge_links.transpose(0, 1, 3, 4, 2, 5)
    clover = clover.transpose(0, 1, 3, 4, 2, 5)
    inputs = (dilution, eigvecs, gauge_links[0])
    chosen, links, carried, *sends, ahead, behind, later = call(
        start_kernel,
        [(6, 8, LANES), (72, LANES), CARRIED] + faces_of(5) + [(6, 8, LANES)] * 2 + [(6, 4, 8, LANES)],
        inputs,
        [(6, 64, LANES)]
        + [pltpu.VMEM(value.shape, value.dtype) for value in inputs]
        + [pltpu.SemaphoreType.DMA((3,))],
        pltpu.MemorySpace.HBM,
    )
    (packed,) = call(clover_kernel, [(144, LANES)], (clover[0],))
    first, slices = exchanged(sends, (ahead, behind))
    psi, carried, *sends, ahead, behind = call(
        first_kernel,
        [FIELD, CARRIED] + faces_of(6) + SLICES,
        (dilution, chosen, links, packed, carried, later, *first, *slices),
        [FIELD],
    )
    second, slices = exchanged(sends, (ahead, behind))
    psi, carried, inner, ahead, behind = call(
        second_kernel,
        [FIELD, CARRIED, FIELD] + SLICES,
        (dilution, chosen, links, packed, psi, carried, *second, *slices),
        [FIELD],
    )
    slices = shifted((ahead, behind))
    inner, *sends = call(
        project_kernel,
        [FIELD, (4, 3, 8, LANES)] + faces_of(2)[2:],
        (links, eigvecs, psi, carried, inner, *slices, *first, *second),
        [FIELD],
    )
    third = [on_line(sends[0])] + [flipped(send, n + 2) for n, send in enumerate(sends[1:])]
    (rows,) = call(line_sum_kernel, [(16, 64)], third)
    blocks = [[16 * n + i for i in range(16)] for n in range(4)]
    parts = lax.all_to_all(rows, "space", 0, 0, axis_index_groups=blocks, tiled=True)
    volume = SITES * lax.axis_size("space")
    reduced = jnp.sum(parts, axis=0) * (1.0 / (3.0 * volume))
    (solutions,) = call(last_kernel, [(24, 8, SITES)], (links, inner, *third), [FIELD])
    return solutions.reshape(2, 4, 3, 1, 8, SITES), reduced.reshape(1, 1, 2, 4, 8)


def solution(mesh):
    in_specs = (
        P(),
        P(None, None, "tm", None, "space"),
        P("tm", None, None, None, None, "space"),
        P("tm", None, None, None, None, "space"),
    )
    out_specs = (P(None, None, None, "tm", None, "space"), P("tm", "space", None, None, None))
    return jax.shard_map(body, mesh=mesh, in_specs=in_specs, out_specs=out_specs, check_vma=False)
```

```python
import functools

import jax
import jax.numpy as jnp
from jax import lax
from jax.experimental import pallas as pl
from jax.experimental.pallas import tpu as pltpu
from jax.sharding import PartitionSpec as P

HOPPING = 0.125
RELAXATION = (0.9, 1.0, 1.1)
SITES = 216
LANES = 256
STRIDES = (36, 6, 1)
SPIN_BLOCKS = (
    ((0.0, -1j), (-1j, 0.0)),
    ((0.0, -1.0), (1.0, 0.0)),
    ((-1j, 0.0), (0.0, 1j)),
    ((1.0, 0.0), (0.0, 1.0)),
)
F32 = jnp.float32


def half(part, spin, colour):
    return (part * 2 + spin) * 3 + colour


def full(part, spin, colour):
    return (part * 4 + spin) * 3 + colour


def rotated(value, shift):
    shift %= LANES
    return value if shift == 0 else pltpu.roll(value, shift, axis=value.ndim - 1)


def add_turned(base, factor, real, imag):
    if factor == 1:
        return base[0] + real, base[1] + imag
    if factor == -1:
        return base[0] - real, base[1] - imag
    if factor == 1j:
        return base[0] - imag, base[1] + real
    return base[0] + imag, base[1] - real


def project(get, direction, parity):
    out = {}
    for spin in range(2):
        row = SPIN_BLOCKS[direction][spin]
        column = 0 if row[0] != 0 else 1
        factor = complex(parity * row[column])
        for colour in range(3):
            base = (get(0, spin, colour), get(1, spin, colour))
            real, imag = add_turned(base, factor, get(0, 2 + column, colour), get(1, 2 + column, colour))
            out[half(0, spin, colour)] = real
            out[half(1, spin, colour)] = imag
    return out


def turned(factor, real, imag):
    if factor == 1:
        return real, imag
    if factor == -1:
        return -real, -imag
    if factor == 1j:
        return -imag, real
    return imag, -real


def lower_of(direction, parity, spin):
    column = 0 if SPIN_BLOCKS[direction][0][spin] != 0 else 1
    return column, complex(parity * complex(SPIN_BLOCKS[direction][column][spin]).conjugate())


def rebuild(total, values, direction, parity):
    for spin in range(2):
        for colour in range(3):
            for part in range(2):
                q = full(part, spin, colour)
                total[q] = total[q] + values[half(part, spin, colour)]
    for spin in range(2):
        column, factor = lower_of(direction, parity, spin)
        for colour in range(3):
            q, r = full(0, 2 + spin, colour), full(1, 2 + spin, colour)
            total[q], total[r] = add_turned(
                (total[q], total[r]), factor, values[half(0, column, colour)], values[half(1, column, colour)]
            )


def rebuilt(values, direction, parity):
    out = {}
    for colour in range(3):
        for spin in range(2):
            for part in range(2):
                out[part, spin, colour] = values[half(part, spin, colour)]
            column, factor = lower_of(direction, parity, spin)
            out[0, 2 + spin, colour], out[1, 2 + spin, colour] = turned(
                factor, values[half(0, column, colour)], values[half(1, column, colour)]
            )
    return out


def link(links, direction, part, row, column):
    at = ((direction * 3 + row) * 3 + column) * 2 + part
    return jnp.broadcast_to(links[at : at + 1, :], (8, LANES))


def color_times(links, direction, values, adjoint):
    out = {}
    for row in range(3):
        for spin in range(2):
            real = imag = None
            for column in range(3):
                at = (column, row) if adjoint else (row, column)
                u_real = link(links, direction, 0, *at)
                u_imag = link(links, direction, 1, *at)
                v_real, v_imag = values[half(0, spin, column)], values[half(1, spin, column)]
                if adjoint:
                    a = u_real * v_real + u_imag * v_imag
                    b = u_real * v_imag - u_imag * v_real
                else:
                    a = u_real * v_real - u_imag * v_imag
                    b = u_real * v_imag + u_imag * v_real
                real = a if real is None else real + a
                imag = b if imag is None else imag + b
            out[half(0, spin, row)] = real
            out[half(1, spin, row)] = imag
    return out


def lane_slots():
    lane = lax.broadcasted_iota(jnp.int32, (8, LANES), 1)
    sixth = lane * 10923 >> 16
    x = sixth * 10923 >> 16
    return x, sixth - 6 * x, lane - 6 * sixth


def even_bits(dimension):
    bits = lax.axis_index("space") >> 2 * (2 - dimension)
    return ((bits ^ bits >> 1) & 1) == 0


def column_of(row):
    square = (8, 8)
    same = lax.broadcasted_iota(jnp.int32, square, 0) == lax.broadcasted_iota(jnp.int32, square, 1)
    return jnp.sum(jnp.where(same, jnp.broadcast_to(row.astype(F32), square), 0.0), axis=1, keepdims=True)


def place(sends, direction, vector, first, second):
    if direction == 0 and len(sends) == 5:
        number = lax.axis_index("space") >> 4
        sends[0][number ^ 1, vector] = first
        sends[0][number ^ 2, vector] = second
    else:
        sends[2 * direction - 6][vector] = first
        sends[2 * direction - 5][vector] = second


def arrived(received, direction, vector):
    if direction == 0 and len(received) == 5:
        number = lax.axis_index("space") >> 4
        first, second = received[0][number ^ 1, vector], received[0][number ^ 2, vector]
    else:
        first, second = received[2 * direction - 6][vector], received[2 * direction - 5][vector]
    low_is_ahead = even_bits(direction)
    return jnp.where(low_is_ahead, first, second), jnp.where(low_is_ahead, second, first)


def packed_low(values, slot, stride):
    out = values[0]
    for r in range(1, 6):
        out = jnp.where(slot == r, rotated(values[r], stride * r), out)
    return out


def packed_high(values, slot, stride):
    out = rotated(values[0], -5 * stride)
    for r in range(1, 6):
        out = jnp.where(slot == r, rotated(values[r], stride * (r - 5)), out)
    return out


def emit_faces(get, carried, sends):
    slots = lane_slots()
    for direction in range(3):
        stride, slot = STRIDES[direction], slots[direction]
        low_is_ahead = even_bits(direction)
        forward = project(get, direction, -1)
        for vector in range(2):
            own = range(6 * vector, 6 * vector + 6)
            low = packed_low([forward[q] for q in own], slot, stride)
            high = packed_high([carried[direction * 12 + q] for q in own], slot, stride)
            place(sends, direction, vector, jnp.where(low_is_ahead, high, low), jnp.where(low_is_ahead, low, high))


def emit_slices(get, links, slices):
    forward = project(get, 3, -1)
    backward = color_times(links, 3, project(get, 3, 1), True)
    for q in range(12):
        slices[0][q] = forward[q]
        slices[1][q] = backward[q]


def carry(get, links, carried):
    for direction in range(3):
        backward = color_times(links, direction, project(get, direction, 1), True)
        for q in range(12):
            carried[direction * 12 + q] = backward[q]


def pick_of(dilution):
    number = jnp.broadcast_to(column_of(dilution[0:1, :]), (8, 64)).astype(jnp.int32)
    return (lax.broadcasted_iota(jnp.int32, (8, 64), 1) == number).astype(F32)


def product(left, right, contracted):
    return lax.dot_general(
        left,
        right,
        ((contracted[:1], contracted[1:]), ((), ())),
        precision=lax.Precision.HIGHEST,
        preferred_element_type=F32,
    )


def masks_of(dilution):
    spins = jnp.broadcast_to(column_of(dilution[1:2, :]), (8, LANES))
    return [(spins == spin).astype(F32) for spin in range(4)]


def source_getter(chosen, masks):
    return lambda part, spin, colour: masks[spin] * chosen[part * 3 + colour]


def start_kernel(dilution, eigvecs, gauge, chosen, links, carried, *rest):
    sends, slices, later, basis = rest[:6], rest[6:8], rest[8], rest[9]
    held, copied = rest[10:13], rest[13]
    copies = [
        pltpu.make_async_copy(source, target, copied.at[n])
        for n, (source, target) in enumerate(zip((dilution, eigvecs, gauge), held))
    ]
    for copy in reversed(copies):
        copy.start()
    links[...] = jnp.zeros_like(links)
    basis[...] = jnp.zeros_like(basis)
    for copy in copies:
        copy.wait()
    dilution, eigvecs, gauge = held
    for direction in range(4):
        for row in range(3):
            for column in range(3):
                at = ((direction * 3 + row) * 3 + column) * 2
                links[at : at + 2, 0:SITES] = gauge[direction, row, column]
    pick = pick_of(dilution)
    for part in range(2):
        for colour in range(3):
            basis[part * 3 + colour, :, 0:SITES] = eigvecs[part, colour]
    for q in range(6):
        chosen[q] = product(pick, basis[q], (1, 0))
    slots = lane_slots()
    for direction in range(4):
        for group in range(-1, 8 if direction < 3 else 0):
            plain = [chosen[q] if group < 0 else basis[q, 8 * group : 8 * group + 8, :] for q in range(6)]
            times = []
            for part in range(2):
                for row in range(3):
                    total = None
                    for column in range(3):
                        u_real = link(links, direction, 0, column, row)
                        u_imag = link(links, direction, 1, column, row)
                        real, imag = plain[column], plain[3 + column]
                        term = u_real * real + u_imag * imag if part == 0 else u_real * imag - u_imag * real
                        total = term if total is None else total + term
                    times.append(total)
            if direction == 3:
                for q in range(6):
                    slices[0][q] = plain[q]
                    slices[1][q] = times[q]
                continue
            stride, slot = STRIDES[direction], slots[direction]
            low_is_ahead = even_bits(direction)
            low = packed_low(plain, slot, stride)
            high = packed_high(times, slot, stride)
            first, second = jnp.where(low_is_ahead, high, low), jnp.where(low_is_ahead, low, high)
            if group < 4:
                place(sends, direction, 1 + group, first, second)
            else:
                later[2 * direction, group - 4] = first
                later[2 * direction + 1, group - 4] = second
    carry(source_getter(chosen, masks_of(dilution)), links, carried)


def clover_kernel(clover, packed):
    packed[...] = jnp.zeros_like(packed)
    for part in range(2):
        for row in range(6):
            for column in range(6):
                at = ((part * 6 + row) * 6 + column) * 2
                packed[at : at + 2, 0:SITES] = clover[part, row, column]


def hop(total, links, get, carried, halos):
    total[...] = jnp.zeros_like(total)
    slots = lane_slots()
    for direction in range(3):
        stride, slot = STRIDES[direction], slots[direction]
        ahead, behind = halos[direction]
        if get is None and ahead is None:
            continue
        forward, backward = {}, {}
        if get is not None:
            for q, value in project(get, direction, -1).items():
                forward[q] = rotated(value, -stride)
                backward[q] = rotated(carried[direction * 12 + q], stride)
        for q in range(12):
            forward[q] = jnp.where(
                slot == 5, 0.0 if ahead is None else ahead[q], 0.0 if get is None else forward[q]
            )
            backward[q] = jnp.where(
                slot == 0, 0.0 if behind is None else behind[q], 0.0 if get is None else backward[q]
            )
        rebuild(total, color_times(links, direction, forward, False), direction, -1)
        rebuild(total, backward, direction, 1)
    ahead, behind = halos[3]
    if ahead is not None:
        rebuild(total, color_times(links, 3, ahead, False), 3, -1)
        rebuild(total, behind, 3, 1)


def slice_halos(slices):
    return [(None, None)] * 3 + [(slices[0], slices[1])]


def field_halos(received):
    halos = []
    for direction in range(3):
        stride = STRIDES[direction]
        ahead, behind = {}, {}
        for vector in range(2):
            from_ahead, from_behind = arrived(received, direction, vector)
            for r in range(6):
                ahead[6 * vector + r] = rotated(from_ahead, stride * (5 - r))
                behind[6 * vector + r] = rotated(from_behind, -stride * r)
        halos.append((ahead, behind))
    return halos


def basis_face(first, second, direction):
    both = [arrived(first, direction, 1 + group) for group in range(4)]
    both += [arrived(second, direction, 2 + group) for group in range(4)]
    return tuple(jnp.concatenate([pair[side] for pair in both], axis=0) for side in range(2))


def source_halos(received, slices, masks):
    halos = []
    for direction in range(4):
        if direction < 3:
            stride = STRIDES[direction]
            from_ahead, from_behind = arrived(received, direction, 0)
            ahead = [rotated(from_ahead, stride * (5 - r)) for r in range(6)]
            behind = [rotated(from_behind, -stride * r) for r in range(6)]
        else:
            ahead, behind = slices
        halos.append(
            (
                project(source_getter(ahead, masks), direction, -1),
                project(source_getter(behind, masks), direction, 1),
            )
        )
    return halos


def relax(weight, get, source, clover, total, store):
    for chiral in range(2):
        for row in range(6):
            real = imag = None
            for column in range(6):
                at = (row * 6 + column) * 2 + chiral
                a_real = jnp.broadcast_to(clover[at : at + 1, :], (8, LANES))
                a_imag = jnp.broadcast_to(clover[72 + at : 73 + at, :], (8, LANES))
                spin, colour = 2 * chiral + column // 3, column % 3
                v_real, v_imag = get(0, spin, colour), get(1, spin, colour)
                a = a_real * v_real - a_imag * v_imag
                b = a_real * v_imag + a_imag * v_real
                real = a if real is None else real + a
                imag = b if imag is None else imag + b
            spin, colour = 2 * chiral + row // 3, row % 3
            for part, applied in ((0, real), (1, imag)):
                q = full(part, spin, colour)
                store[q] = get(part, spin, colour) + weight * (
                    source(part, spin, colour) - (applied - HOPPING * total[q])
                )


def getter(ref):
    return lambda part, spin, colour: ref[full(part, spin, colour)]


def first_kernel(dilution, chosen, links, clover, carried_in, later, *rest):
    received, slices, psi, carried = rest[:6], rest[6:8], rest[8], rest[9]
    sends, next_slices, total = rest[10:16], rest[16:18], rest[18]
    masks = masks_of(dilution)
    source = source_getter(chosen, masks)
    hop(total, links, source, carried_in, source_halos(received, slices, masks))
    relax(RELAXATION[0], source, source, clover, total, psi)
    carry(getter(psi), links, carried)
    emit_faces(getter(psi), carried, sends)
    for direction in range(3):
        for group in range(4):
            place(sends, direction, 2 + group, later[2 * direction, group], later[2 * direction + 1, group])
    emit_slices(getter(psi), links, next_slices)


def projected_rows(values, place_at):
    rows = []
    for part in range(2):
        for spin in range(4):
            real = [values(part, spin, colour) for colour in range(3)]
            other = [values(1 - part, spin, colour) for colour in range(3)]
            if part == 1:
                other = [-value for value in other]
            rows.append(place_at(real, other))
    return rows


def projections(eigvecs, inner, psi, carried, first, second):
    summed = None
    rows = projected_rows(getter(inner), lambda real, other: real + other)
    for part in range(2):
        for colour in range(3):
            field = jnp.concatenate([row[3 * part + colour][:, 0:SITES] for row in rows], axis=0)
            term = product(eigvecs[part, colour], field, (1, 1))
            summed = term if summed is None else summed + term
    slots = lane_slots()
    inside = lax.broadcasted_iota(jnp.int32, (8, LANES), 1) < SITES
    faces = None
    for direction in range(3):
        stride, slot = STRIDES[direction], slots[direction]
        low = rebuilt(project(getter(psi), direction, -1), direction, -1)
        high = rebuilt([carried[direction * 12 + q] for q in range(12)], direction, 1)
        from_ahead, from_behind = basis_face(first, second, direction)
        for values, face, pack in ((low, from_behind, packed_low), (high, from_ahead, packed_high)):
            rows = projected_rows(
                lambda part, spin, colour: values[part, spin, colour],
                lambda real, other: jnp.where(inside, pack(real + other, slot, stride), 0.0),
            )
            term = product(face, jnp.concatenate(rows, axis=0), (1, 1))
            faces = term if faces is None else faces + term
    return summed + (RELAXATION[2] * HOPPING) * faces


def second_kernel(dilution, chosen, links, clover, spinor, carried_in, *rest):
    received, slices, (psi, carried, inner), next_slices = rest[:6], rest[6:8], rest[8:11], rest[11:13]
    (x_faces, *sends), total = rest[13:18], rest[18]
    source = source_getter(chosen, masks_of(dilution))
    hop(total, links, getter(spinor), carried_in, field_halos(received) + [(slices[0], slices[1])])
    relax(RELAXATION[1], getter(spinor), source, clover, total, psi)
    emit_slices(getter(psi), links, next_slices)
    carry(getter(psi), links, carried)
    emit_faces(getter(psi), carried, [x_faces.at[0], x_faces.at[1], *sends])
    hop(total, links, getter(psi), carried, [(None, None)] * 4)
    relax(RELAXATION[2], getter(psi), source, clover, total, inner)


def project_kernel(links, eigvecs, psi, carried, inner_in, *rest):
    slices, first, second, faces = rest[:2], rest[2:8], rest[8:14], rest[14:17]
    inner, partial, faces_out, total = rest[17], rest[18], rest[19:22], rest[22]
    hop(total, links, None, None, slice_halos(slices))
    for q in range(24):
        inner[q] = inner_in[q] + (RELAXATION[2] * HOPPING) * total[q]
    for face, out in zip(faces, faces_out):
        out[...] = face[...]
    at = lax.broadcasted_iota(jnp.int32, (128, 64), 0)
    wanted = jnp.where((at & 7) < 4, (at & 7) << 4 | at >> 3, 64)
    order = (lax.broadcasted_iota(jnp.int32, (128, 64), 1) == wanted).astype(F32)
    partial[...] = jnp.zeros_like(partial)
    partial[:, 0:64] = product(order, projections(eigvecs, inner, psi, carried, first, second), (1, 0))


def far_kernel(parts, x_faces, out):
    out[...] = jnp.zeros_like(out)
    number = lax.axis_index("space") >> 4
    out[number ^ 1, 0:2] = x_faces[0]
    out[number ^ 2, 0:2] = x_faces[1]
    rows = parts[0]
    for i in range(1, 16):
        rows = rows + parts[i]
    for n in range(4):
        out[n, 2, 0:1, 0:128] = rows[n : n + 1, :]


def last_kernel(scale, links, inner, *rest):
    received, solutions, reduced, total = rest[:5], rest[5], rest[6], rest[7]
    hop(total, links, None, None, field_halos(received) + [(None, None)])
    for q in range(24):
        solutions[q] = (inner[q] + (RELAXATION[2] * HOPPING) * total[q])[:, 0:SITES]
    row = received[0][0, 2, 0:1, 0:64]
    for n in range(1, 4):
        row = row + received[0][n, 2, 0:1, 0:64]
    column = lax.broadcasted_iota(jnp.int32, (8, 64), 1)
    spread = jnp.where(column >> 3 == lax.broadcasted_iota(jnp.int32, (8, 64), 0), row * scale, 0.0)
    entry = lax.broadcasted_iota(jnp.int32, (64, 8), 0) & 7
    reduced[...] = product(spread, (entry == lax.broadcasted_iota(jnp.int32, (64, 8), 1)).astype(F32), (1, 0))


def call(kernel, outs, args, scratch=(), place=pltpu.VMEM):
    vmem = pl.BlockSpec(memory_space=pltpu.VMEM)
    return pl.pallas_call(
        kernel,
        out_shape=[jax.ShapeDtypeStruct(shape, F32) for shape in outs],
        in_specs=[pl.BlockSpec(memory_space=place)] * len(args),
        out_specs=[vmem] * len(outs),
        scratch_shapes=[pltpu.VMEM(shape, F32) if isinstance(shape, tuple) else shape for shape in scratch],
        compiler_params=pltpu.CompilerParams(vmem_limit_bytes=16 << 20),
    )(*args)


SLICES = [(12, 8, LANES)] * 2
FIELD = (24, 8, LANES)
CARRIED = (36, 8, LANES)


def faces_of(vectors):
    return [(vectors, 8, LANES)] * 6


BITS = (4, 5, 2, 3, 0, 1)


def flipped(value, n):
    return lax.ppermute(value, "space", [(i, i ^ 1 << BITS[n]) for i in range(lax.axis_size("space"))])


def on_line(value):
    lines = [[i + 16 * n for n in range(4)] for i in range(16)]
    return lax.all_to_all(value, "space", 0, 0, axis_index_groups=lines, tiled=True)


def shifted(slices):
    length = lax.axis_size("tm")
    out = []
    for n, by in enumerate((-1, 1)):
        out.append(lax.ppermute(slices[n], "tm", [(i, (i + by) % length) for i in range(length)]))
    return out


def exchanged(sends, slices):
    return [flipped(send, n) for n, send in enumerate(sends)], shifted(slices)


def body(dilution, eigvecs, gauge_links, clover):
    eigvecs = eigvecs[:, :, 0]
    dilution = dilution.T
    gauge_links = gauge_links.transpose(0, 1, 3, 4, 2, 5)
    clover = clover.transpose(0, 1, 3, 4, 2, 5)
    inputs = (dilution, eigvecs, gauge_links[0])
    chosen, links, carried, *sends, ahead, behind, later = call(
        start_kernel,
        [(6, 8, LANES), (72, LANES), CARRIED] + faces_of(5) + [(6, 8, LANES)] * 2 + [(6, 4, 8, LANES)],
        inputs,
        [(6, 64, LANES)]
        + [pltpu.VMEM(value.shape, value.dtype) for value in inputs]
        + [pltpu.SemaphoreType.DMA((3,))],
        pltpu.MemorySpace.HBM,
    )
    (packed,) = call(clover_kernel, [(144, LANES)], (clover[0],))
    first, slices = exchanged(sends, (ahead, behind))
    psi, carried, *sends, ahead, behind = call(
        first_kernel,
        [FIELD, CARRIED] + faces_of(6) + SLICES,
        (dilution, chosen, links, packed, carried, later, *first, *slices),
        [FIELD],
    )
    second, slices = exchanged(sends, (ahead, behind))
    psi, carried, inner, ahead, behind, x_faces, *faces = call(
        second_kernel,
        [FIELD, CARRIED, FIELD] + SLICES + [(2, 2, 8, LANES)] + faces_of(2)[2:],
        (dilution, chosen, links, packed, psi, carried, *second, *slices),
        [FIELD],
    )
    slices = shifted((ahead, behind))
    y_far = flipped(faces[1], 3)
    inner, partial, *faces = call(
        project_kernel,
        [FIELD, (128, 128)] + faces_of(2)[:3],
        (links, eigvecs, psi, carried, inner, *slices, *first, *second, faces[0], faces[2], faces[3]),
        [FIELD],
    )
    blocks = [[16 * n + i for i in range(16)] for n in range(4)]
    parts = lax.all_to_all(
        partial.reshape(16, 8, 128), "space", 0, 0, axis_index_groups=blocks, tiled=True
    )
    near = [flipped(face, n) for face, n in zip(faces, (2, 4, 5))]
    (far,) = call(far_kernel, [(4, 3, 8, LANES)], (parts, x_faces))
    third = [on_line(far), near[0], y_far, near[1], near[2]]
    scale = 1.0 / (3.0 * SITES * lax.axis_size("space"))
    solutions, reduced = call(
        functools.partial(last_kernel, scale), [(24, 8, SITES), (8, 8)], (links, inner, *third), [FIELD]
    )
    return solutions.reshape(2, 4, 3, 1, 8, SITES), reduced.reshape(1, 1, 2, 4, 8)


def solution(mesh):
    in_specs = (
        P(),
        P(None, None, "tm", None, "space"),
        P("tm", None, None, None, None, "space"),
        P("tm", None, None, None, None, "space"),
    )
    out_specs = (P(None, None, None, "tm", None, "space"), P("tm", "space", None, None, None))
    return jax.shard_map(body, mesh=mesh, in_specs=in_specs, out_specs=out_specs, check_vma=False)
```

```python
import functools

import jax
import jax.numpy as jnp
from jax import lax
from jax.experimental import pallas as pl
from jax.experimental.pallas import tpu as pltpu
from jax.sharding import PartitionSpec as P

HOPPING = 0.125
RELAXATION = (0.9, 1.0, 1.1)
SITES = 216
LANES = 256
STRIDES = (36, 6, 1)
SPIN_BLOCKS = (
    ((0.0, -1j), (-1j, 0.0)),
    ((0.0, -1.0), (1.0, 0.0)),
    ((-1j, 0.0), (0.0, 1j)),
    ((1.0, 0.0), (0.0, 1.0)),
)
F32 = jnp.float32


def half(part, spin, colour):
    return (part * 2 + spin) * 3 + colour


def full(part, spin, colour):
    return (part * 4 + spin) * 3 + colour


def rotated(value, shift):
    shift %= LANES
    return value if shift == 0 else pltpu.roll(value, shift, axis=value.ndim - 1)


def add_turned(base, factor, real, imag):
    if factor == 1:
        return base[0] + real, base[1] + imag
    if factor == -1:
        return base[0] - real, base[1] - imag
    if factor == 1j:
        return base[0] - imag, base[1] + real
    return base[0] + imag, base[1] - real


def project(get, direction, parity):
    out = {}
    for spin in range(2):
        row = SPIN_BLOCKS[direction][spin]
        column = 0 if row[0] != 0 else 1
        factor = complex(parity * row[column])
        for colour in range(3):
            base = (get(0, spin, colour), get(1, spin, colour))
            real, imag = add_turned(base, factor, get(0, 2 + column, colour), get(1, 2 + column, colour))
            out[half(0, spin, colour)] = real
            out[half(1, spin, colour)] = imag
    return out


def turned(factor, real, imag):
    if factor == 1:
        return real, imag
    if factor == -1:
        return -real, -imag
    if factor == 1j:
        return -imag, real
    return imag, -real


def lower_of(direction, parity, spin):
    column = 0 if SPIN_BLOCKS[direction][0][spin] != 0 else 1
    return column, complex(parity * complex(SPIN_BLOCKS[direction][column][spin]).conjugate())


def rebuild(total, values, direction, parity):
    for spin in range(2):
        for colour in range(3):
            for part in range(2):
                q = full(part, spin, colour)
                total[q] = total[q] + values[half(part, spin, colour)]
    for spin in range(2):
        column, factor = lower_of(direction, parity, spin)
        for colour in range(3):
            q, r = full(0, 2 + spin, colour), full(1, 2 + spin, colour)
            total[q], total[r] = add_turned(
                (total[q], total[r]), factor, values[half(0, column, colour)], values[half(1, column, colour)]
            )


def rebuilt(values, direction, parity):
    out = {}
    for colour in range(3):
        for spin in range(2):
            for part in range(2):
                out[part, spin, colour] = values[half(part, spin, colour)]
            column, factor = lower_of(direction, parity, spin)
            out[0, 2 + spin, colour], out[1, 2 + spin, colour] = turned(
                factor, values[half(0, column, colour)], values[half(1, column, colour)]
            )
    return out


def link(links, direction, part, row, column):
    at = ((direction * 3 + row) * 3 + column) * 2 + part
    return jnp.broadcast_to(links[at : at + 1, :], (8, LANES))


def color_times(links, direction, values, adjoint):
    out = {}
    for row in range(3):
        for spin in range(2):
            real = imag = None
            for column in range(3):
                at = (column, row) if adjoint else (row, column)
                u_real = link(links, direction, 0, *at)
                u_imag = link(links, direction, 1, *at)
                v_real, v_imag = values[half(0, spin, column)], values[half(1, spin, column)]
                if adjoint:
                    a = u_real * v_real + u_imag * v_imag
                    b = u_real * v_imag - u_imag * v_real
                else:
                    a = u_real * v_real - u_imag * v_imag
                    b = u_real * v_imag + u_imag * v_real
                real = a if real is None else real + a
                imag = b if imag is None else imag + b
            out[half(0, spin, row)] = real
            out[half(1, spin, row)] = imag
    return out


def lane_slots():
    lane = lax.broadcasted_iota(jnp.int32, (8, LANES), 1)
    sixth = lane * 10923 >> 16
    x = sixth * 10923 >> 16
    return x, sixth - 6 * x, lane - 6 * sixth


def even_bits(dimension):
    bits = lax.axis_index("space") >> 2 * (2 - dimension)
    return ((bits ^ bits >> 1) & 1) == 0


def column_of(row):
    square = (8, 8)
    same = lax.broadcasted_iota(jnp.int32, square, 0) == lax.broadcasted_iota(jnp.int32, square, 1)
    return jnp.sum(jnp.where(same, jnp.broadcast_to(row.astype(F32), square), 0.0), axis=1, keepdims=True)


def place(sends, direction, vector, first, second):
    sends[2 * direction][vector] = first
    sends[2 * direction + 1][vector] = second


def arrived(received, direction, vector):
    first, second = received[2 * direction][vector], received[2 * direction + 1][vector]
    low_is_ahead = even_bits(direction)
    return jnp.where(low_is_ahead, first, second), jnp.where(low_is_ahead, second, first)


def packed_low(values, slot, stride):
    out = values[0]
    for r in range(1, 6):
        out = jnp.where(slot == r, rotated(values[r], stride * r), out)
    return out


def packed_high(values, slot, stride):
    out = rotated(values[0], -5 * stride)
    for r in range(1, 6):
        out = jnp.where(slot == r, rotated(values[r], stride * (r - 5)), out)
    return out


def emit_faces(get, carried, sends):
    slots = lane_slots()
    for direction in range(3):
        stride, slot = STRIDES[direction], slots[direction]
        low_is_ahead = even_bits(direction)
        forward = project(get, direction, -1)
        for vector in range(2):
            own = range(6 * vector, 6 * vector + 6)
            low = packed_low([forward[q] for q in own], slot, stride)
            high = packed_high([carried[direction * 12 + q] for q in own], slot, stride)
            place(sends, direction, vector, jnp.where(low_is_ahead, high, low), jnp.where(low_is_ahead, low, high))


def emit_slices(get, links, slices):
    forward = project(get, 3, -1)
    backward = color_times(links, 3, project(get, 3, 1), True)
    for q in range(12):
        slices[0][q] = forward[q]
        slices[1][q] = backward[q]


def carry(get, links, carried):
    for direction in range(3):
        backward = color_times(links, direction, project(get, direction, 1), True)
        for q in range(12):
            carried[direction * 12 + q] = backward[q]


def pick_of(dilution):
    number = jnp.broadcast_to(column_of(dilution[0:1, :]), (8, 64)).astype(jnp.int32)
    return (lax.broadcasted_iota(jnp.int32, (8, 64), 1) == number).astype(F32)


def product(left, right, contracted):
    return lax.dot_general(
        left,
        right,
        ((contracted[:1], contracted[1:]), ((), ())),
        precision=lax.Precision.HIGHEST,
        preferred_element_type=F32,
    )


def masks_of(dilution):
    spins = jnp.broadcast_to(column_of(dilution[1:2, :]), (8, LANES))
    return [(spins == spin).astype(F32) for spin in range(4)]


def source_getter(chosen, masks):
    return lambda part, spin, colour: masks[spin] * chosen[part * 3 + colour]


def start_kernel(dilution, eigvecs, gauge, chosen, links, carried, *rest):
    sends, slices, later, basis = rest[:6], rest[6:8], rest[8], rest[9]
    held, copied = rest[10:13], rest[13]
    copies = [
        pltpu.make_async_copy(source, target, copied.at[n])
        for n, (source, target) in enumerate(zip((dilution, eigvecs, gauge), held))
    ]
    for copy in reversed(copies):
        copy.start()
    links[...] = jnp.zeros_like(links)
    basis[...] = jnp.zeros_like(basis)
    for copy in copies:
        copy.wait()
    dilution, eigvecs, gauge = held
    for direction in range(4):
        for row in range(3):
            for column in range(3):
                at = ((direction * 3 + row) * 3 + column) * 2
                links[at : at + 2, 0:SITES] = gauge[direction, row, column]
    pick = pick_of(dilution)
    for part in range(2):
        for colour in range(3):
            basis[part * 3 + colour, :, 0:SITES] = eigvecs[part, colour]
    for q in range(6):
        chosen[q] = product(pick, basis[q], (1, 0))
    slots = lane_slots()
    for direction in range(4):
        for group in range(-1, 8 if direction < 3 else 0):
            plain = [chosen[q] if group < 0 else basis[q, 8 * group : 8 * group + 8, :] for q in range(6)]
            times = []
            for part in range(2):
                for row in range(3):
                    total = None
                    for column in range(3):
                        u_real = link(links, direction, 0, column, row)
                        u_imag = link(links, direction, 1, column, row)
                        real, imag = plain[column], plain[3 + column]
                        term = u_real * real + u_imag * imag if part == 0 else u_real * imag - u_imag * real
                        total = term if total is None else total + term
                    times.append(total)
            if direction == 3:
                for q in range(6):
                    slices[0][q] = plain[q]
                    slices[1][q] = times[q]
                continue
            stride, slot = STRIDES[direction], slots[direction]
            low_is_ahead = even_bits(direction)
            low = packed_low(plain, slot, stride)
            high = packed_high(times, slot, stride)
            first, second = jnp.where(low_is_ahead, high, low), jnp.where(low_is_ahead, low, high)
            if group < 4:
                place(sends, direction, 1 + group, first, second)
            else:
                later[2 * direction, group - 4] = first
                later[2 * direction + 1, group - 4] = second
    carry(source_getter(chosen, masks_of(dilution)), links, carried)


def clover_kernel(clover, packed):
    packed[...] = jnp.zeros_like(packed)
    for part in range(2):
        for row in range(6):
            for column in range(6):
                at = ((part * 6 + row) * 6 + column) * 2
                packed[at : at + 2, 0:SITES] = clover[part, row, column]


def hop(total, links, get, carried, halos):
    total[...] = jnp.zeros_like(total)
    slots = lane_slots()
    for direction in range(3):
        stride, slot = STRIDES[direction], slots[direction]
        ahead, behind = halos[direction]
        if get is None and ahead is None:
            continue
        forward, backward = {}, {}
        if get is not None:
            for q, value in project(get, direction, -1).items():
                forward[q] = rotated(value, -stride)
                backward[q] = rotated(carried[direction * 12 + q], stride)
        for q in range(12):
            forward[q] = jnp.where(
                slot == 5, 0.0 if ahead is None else ahead[q], 0.0 if get is None else forward[q]
            )
            backward[q] = jnp.where(
                slot == 0, 0.0 if behind is None else behind[q], 0.0 if get is None else backward[q]
            )
        rebuild(total, color_times(links, direction, forward, False), direction, -1)
        rebuild(total, backward, direction, 1)
    ahead, behind = halos[3]
    if ahead is not None:
        rebuild(total, color_times(links, 3, ahead, False), 3, -1)
        rebuild(total, behind, 3, 1)


def slice_halos(slices):
    return [(None, None)] * 3 + [(slices[0], slices[1])]


def field_halos(received):
    halos = []
    for direction in range(3):
        stride = STRIDES[direction]
        ahead, behind = {}, {}
        for vector in range(2):
            from_ahead, from_behind = arrived(received, direction, vector)
            for r in range(6):
                ahead[6 * vector + r] = rotated(from_ahead, stride * (5 - r))
                behind[6 * vector + r] = rotated(from_behind, -stride * r)
        halos.append((ahead, behind))
    return halos


def basis_face(first, second, direction):
    both = [arrived(first, direction, 1 + group) for group in range(4)]
    both += [arrived(second, direction, 2 + group) for group in range(4)]
    return tuple(jnp.concatenate([pair[side] for pair in both], axis=0) for side in range(2))


def source_halos(received, slices, masks):
    halos = []
    for direction in range(4):
        if direction < 3:
            stride = STRIDES[direction]
            from_ahead, from_behind = arrived(received, direction, 0)
            ahead = [rotated(from_ahead, stride * (5 - r)) for r in range(6)]
            behind = [rotated(from_behind, -stride * r) for r in range(6)]
        else:
            ahead, behind = slices
        halos.append(
            (
                project(source_getter(ahead, masks), direction, -1),
                project(source_getter(behind, masks), direction, 1),
            )
        )
    return halos


def relax(weight, get, source, clover, total, store):
    for chiral in range(2):
        for row in range(6):
            real = imag = None
            for column in range(6):
                at = (row * 6 + column) * 2 + chiral
                a_real = jnp.broadcast_to(clover[at : at + 1, :], (8, LANES))
                a_imag = jnp.broadcast_to(clover[72 + at : 73 + at, :], (8, LANES))
                spin, colour = 2 * chiral + column // 3, column % 3
                v_real, v_imag = get(0, spin, colour), get(1, spin, colour)
                a = a_real * v_real - a_imag * v_imag
                b = a_real * v_imag + a_imag * v_real
                real = a if real is None else real + a
                imag = b if imag is None else imag + b
            spin, colour = 2 * chiral + row // 3, row % 3
            for part, applied in ((0, real), (1, imag)):
                q = full(part, spin, colour)
                store[q] = get(part, spin, colour) + weight * (
                    source(part, spin, colour) - (applied - HOPPING * total[q])
                )


def getter(ref):
    return lambda part, spin, colour: ref[full(part, spin, colour)]


def first_kernel(dilution, chosen, links, clover, carried_in, later, *rest):
    received, slices, psi, carried = rest[:6], rest[6:8], rest[8], rest[9]
    sends, next_slices, total = rest[10:16], rest[16:18], rest[18]
    masks = masks_of(dilution)
    source = source_getter(chosen, masks)
    hop(total, links, source, carried_in, source_halos(received, slices, masks))
    relax(RELAXATION[0], source, source, clover, total, psi)
    carry(getter(psi), links, carried)
    emit_faces(getter(psi), carried, sends)
    for direction in range(3):
        for group in range(4):
            place(sends, direction, 2 + group, later[2 * direction, group], later[2 * direction + 1, group])
    emit_slices(getter(psi), links, next_slices)


def projected_rows(values, place_at):
    rows = []
    for part in range(2):
        for spin in range(4):
            real = [values(part, spin, colour) for colour in range(3)]
            other = [values(1 - part, spin, colour) for colour in range(3)]
            if part == 1:
                other = [-value for value in other]
            rows.append(place_at(real, other))
    return rows


def projections(eigvecs, inner, psi, carried, first, second):
    summed = None
    rows = projected_rows(getter(inner), lambda real, other: real + other)
    for part in range(2):
        for colour in range(3):
            field = jnp.concatenate([row[3 * part + colour][:, 0:SITES] for row in rows], axis=0)
            term = product(eigvecs[part, colour], field, (1, 1))
            summed = term if summed is None else summed + term
    slots = lane_slots()
    inside = lax.broadcasted_iota(jnp.int32, (8, LANES), 1) < SITES
    faces = None
    for direction in range(3):
        stride, slot = STRIDES[direction], slots[direction]
        low = rebuilt(project(getter(psi), direction, -1), direction, -1)
        high = rebuilt([carried[direction * 12 + q] for q in range(12)], direction, 1)
        from_ahead, from_behind = basis_face(first, second, direction)
        for values, face, pack in ((low, from_behind, packed_low), (high, from_ahead, packed_high)):
            rows = projected_rows(
                lambda part, spin, colour: values[part, spin, colour],
                lambda real, other: jnp.where(inside, pack(real + other, slot, stride), 0.0),
            )
            term = product(face, jnp.concatenate(rows, axis=0), (1, 1))
            faces = term if faces is None else faces + term
    return summed + (RELAXATION[2] * HOPPING) * faces


def second_kernel(dilution, chosen, links, clover, spinor, carried_in, *rest):
    received, slices, (psi, carried, inner), next_slices = rest[:6], rest[6:8], rest[8:11], rest[11:13]
    sends, total = rest[13:19], rest[19]
    source = source_getter(chosen, masks_of(dilution))
    hop(total, links, getter(spinor), carried_in, field_halos(received) + [(slices[0], slices[1])])
    relax(RELAXATION[1], getter(spinor), source, clover, total, psi)
    emit_slices(getter(psi), links, next_slices)
    carry(getter(psi), links, carried)
    emit_faces(getter(psi), carried, sends)
    hop(total, links, getter(psi), carried, [(None, None)] * 4)
    relax(RELAXATION[2], getter(psi), source, clover, total, inner)


def project_kernel(links, eigvecs, psi, carried, inner_in, *rest):
    slices, first, second, inner, partial, total = rest[:2], rest[2:8], rest[8:14], rest[14], rest[15], rest[16]
    hop(total, links, None, None, slice_halos(slices))
    for q in range(24):
        inner[q] = inner_in[q] + (RELAXATION[2] * HOPPING) * total[q]
    partial[...] = projections(eigvecs, inner, psi, carried, first, second)


def last_kernel(scale, links, inner, parts, *rest):
    received, solutions, reduced, total = rest[:6], rest[6], rest[7], rest[8]
    hop(total, links, None, None, field_halos(received) + [(None, None)])
    for q in range(24):
        solutions[q] = (inner[q] + (RELAXATION[2] * HOPPING) * total[q])[:, 0:SITES]
    row = jnp.sum(parts[...], axis=0, keepdims=True) * scale
    column = lax.broadcasted_iota(jnp.int32, (8, 64), 1)
    spread = jnp.where(column >> 3 == lax.broadcasted_iota(jnp.int32, (8, 64), 0), row, 0.0)
    entry = lax.broadcasted_iota(jnp.int32, (64, 8), 0) & 7
    reduced[...] = product(spread, (entry == lax.broadcasted_iota(jnp.int32, (64, 8), 1)).astype(F32), (1, 0))


def call(kernel, outs, args, scratch=(), place=pltpu.VMEM):
    vmem = pl.BlockSpec(memory_space=pltpu.VMEM)
    return pl.pallas_call(
        kernel,
        out_shape=[jax.ShapeDtypeStruct(shape, F32) for shape in outs],
        in_specs=[pl.BlockSpec(memory_space=place)] * len(args),
        out_specs=[vmem] * len(outs),
        scratch_shapes=[pltpu.VMEM(shape, F32) if isinstance(shape, tuple) else shape for shape in scratch],
        compiler_params=pltpu.CompilerParams(vmem_limit_bytes=16 << 20),
    )(*args)


SLICES = [(12, 8, LANES)] * 2
FIELD = (24, 8, LANES)
CARRIED = (36, 8, LANES)


def faces_of(vectors):
    return [(vectors, 8, LANES)] * 6


BITS = (4, 5, 2, 3, 0, 1)


def flipped(value, n):
    return lax.ppermute(value, "space", [(i, i ^ 1 << BITS[n]) for i in range(lax.axis_size("space"))])


def shifted(slices):
    length = lax.axis_size("tm")
    out = []
    for n, by in enumerate((-1, 1)):
        out.append(lax.ppermute(slices[n], "tm", [(i, (i + by) % length) for i in range(length)]))
    return out


def exchanged(sends, slices):
    return [flipped(send, n) for n, send in enumerate(sends)], shifted(slices)


def body(dilution, eigvecs, gauge_links, clover):
    eigvecs = eigvecs[:, :, 0]
    dilution = dilution.T
    gauge_links = gauge_links.transpose(0, 1, 3, 4, 2, 5)
    clover = clover.transpose(0, 1, 3, 4, 2, 5)
    inputs = (dilution, eigvecs, gauge_links[0])
    chosen, links, carried, *sends, ahead, behind, later = call(
        start_kernel,
        [(6, 8, LANES), (72, LANES), CARRIED] + faces_of(5) + [(6, 8, LANES)] * 2 + [(6, 4, 8, LANES)],
        inputs,
        [(6, 64, LANES)]
        + [pltpu.VMEM(value.shape, value.dtype) for value in inputs]
        + [pltpu.SemaphoreType.DMA((3,))],
        pltpu.MemorySpace.HBM,
    )
    (packed,) = call(clover_kernel, [(144, LANES)], (clover[0],))
    first, slices = exchanged(sends, (ahead, behind))
    psi, carried, *sends, ahead, behind = call(
        first_kernel,
        [FIELD, CARRIED] + faces_of(6) + SLICES,
        (dilution, chosen, links, packed, carried, later, *first, *slices),
        [FIELD],
    )
    second, slices = exchanged(sends, (ahead, behind))
    psi, carried, inner, ahead, behind, *sends = call(
        second_kernel,
        [FIELD, CARRIED, FIELD] + SLICES + faces_of(2),
        (dilution, chosen, links, packed, psi, carried, *second, *slices),
        [FIELD],
    )
    third, slices = exchanged(sends, (ahead, behind))
    inner, partial = call(
        project_kernel, [FIELD, (64, 64)], (links, eigvecs, psi, carried, inner, *slices, *first, *second), [FIELD]
    )
    parts = lax.all_to_all(partial, "space", 0, 0, tiled=True)
    scale = 1.0 / (3.0 * SITES * lax.axis_size("space"))
    solutions, reduced = call(
        functools.partial(last_kernel, scale), [(24, 8, SITES), (8, 8)], (links, inner, parts, *third), [FIELD]
    )
    return solutions.reshape(2, 4, 3, 1, 8, SITES), reduced.reshape(1, 1, 2, 4, 8)


def solution(mesh):
    in_specs = (
        P(),
        P(None, None, "tm", None, "space"),
        P("tm", None, None, None, None, "space"),
        P("tm", None, None, None, None, "space"),
    )
    out_specs = (P(None, None, None, "tm", None, "space"), P("tm", "space", None, None, None))
    return jax.shard_map(body, mesh=mesh, in_specs=in_specs, out_specs=out_specs, check_vma=False)
```
